128 devices in a mesh: kpair: 4 (over x_hi, core), band: 2 (over x_lo), pencil: 16 (over z, y).
Axes of the slice: x: 4 (x_hi: 2, x_lo: 2; x = x_hi * 2 + x_lo), y: 4, z: 4, core: 2. Of those that a mesh axis runs over, the one named last changes fastest.
Arguments:
- orbitals: float32 [2, 4, 2, 96, 9216], P(None, 'kpair', 'band', 'pencil'), may hold values from -6 to 6
- kcoords: int32 [4, 3], replicated, may hold values from 0 to 3, as said below
Outputs:
- exchange_vectors: float32 [2, 4, 2, 96, 9216], P(None, 'kpair', 'band', 'pencil')
The draws below stay inside these ranges and needn't reach their ends.
Inputs may be any that keep to these rules, and one draw needn't show every extreme that they name: `kcoords`: each row is a point of a 4 x 4 x 4 k-point grid given by three integer coordinates; the rows are distinct.
All inputs are finite; a program needn't handle non-finite values.
Results may differ from the reference program's by a relative error of at most 0.0001.
Values sent between devices are 32-bit elements; how exact they have to be, the bound alone decides.
No kernel may reach another device: no remote copies, remote signals or barrier semaphores. Data moves between devices by JAX's collectives and lax.ppermute only.
A program may use at most 128 MiB of HBM per device.

```python
import math
import jax
import jax.numpy as jnp
from jax import lax

GRID = 96
NB = 2
KPTS = 4


def draw_kcoords(key, part):
    shuffled = jax.random.permutation(key, 64)
    place_high = jnp.argmax(shuffled == 63)
    shuffled = shuffled.at[place_high].set(shuffled[0]).at[0].set(63)
    place_low = jnp.argmax(shuffled == 0)
    shuffled = shuffled.at[place_low].set(shuffled[1]).at[1].set(0)
    chosen = shuffled[:KPTS]
    return jnp.stack([chosen // 16, chosen // 4 % 4, chosen % 4], axis=1).astype(jnp.int32)


def steps_of(key, shape, shards, low, largest):
    gain = 1.0
    for position, parts in shards:
        heights = jax.random.uniform(jax.random.fold_in(jax.random.fold_in(key, 6), position), (parts,), jnp.float32, low / len(shards), largest / len(shards))
        gain = gain * jnp.repeat(jnp.exp(heights), shape[position] // parts).reshape((-1,) + (1,) * (len(shape) - 1 - position))
    return gain


def normal_values(rng, shape, width, reach, shards=(), kind=jnp.bfloat16):
    values = width * jax.random.normal(rng, shape, jnp.float32)
    if shards:
        values = values * steps_of(rng, shape, shards, -0.22, 0.18)
    return jnp.clip(values, -reach, reach).astype(kind)


def setup_inputs(seed: int = 0) -> dict:
    seeds = jax.random.split(jax.random.key(seed), 3)
    return {
        "orbitals": normal_values(seeds[0], (2, KPTS, NB, GRID, GRID * GRID), 1.0, 6.0, ((1, 4), (2, 2), (3, 16)), jnp.float32),
        "kcoords": draw_kcoords(jax.random.fold_in(seeds[2], 71), 0),
    }


screening = 0.5


def frequencies():
    positions = jnp.arange(GRID)
    return jnp.where(positions < GRID // 2, positions, positions - GRID).astype(jnp.float32)


def coulomb_grid(shift_vector, along_x, along_y, along_z):
    squared = (along_x[:, None, None] + shift_vector[0]) ** 2
    squared = squared + (along_y[None, :, None] + shift_vector[1]) ** 2
    squared = squared + (along_z[None, None, :] + shift_vector[2]) ** 2
    radius = GRID // 2 - 1
    factor = (2.0 * math.pi / GRID) ** 2
    return jnp.where(squared <= radius * radius, 4.0 * math.pi / (factor * squared + screening), 0.0)


def reference(orbitals, kcoords):
    kpts = kcoords.shape[0]
    fields = lax.complex(orbitals[0], orbitals[1]).reshape(kpts, NB, GRID, GRID, GRID)
    frequency = frequencies()
    coords = kcoords.astype(jnp.float32) * 0.25
    weight = -1.0 / (kpts * NB)
    results = []
    for kpoint in range(kpts):
        own_fields = fields[kpoint]
        running = jnp.zeros_like(own_fields)
        for target in range(kpts):
            far_fields = fields[target]
            coulomb = coulomb_grid(coords[kpoint] - coords[target], frequency, frequency, frequency)
            density = jnp.conj(far_fields)[None] * own_fields[:, None]
            spectrum = jnp.fft.fftn(density, axes=(2, 3, 4))
            potential = jnp.fft.ifftn(coulomb * spectrum, axes=(2, 3, 4))
            running = running + jnp.sum(far_fields[None] * potential, axis=1)
        results.append(weight * running)
    stacked = jnp.stack(results)
    output = jnp.stack([jnp.real(stacked), jnp.imag(stacked)])
    return output.reshape(2, kpts, NB, GRID, GRID * GRID).astype(jnp.float32)
```

```python
import math

import jax
import jax.numpy as jnp
import numpy as np
from jax import lax
from jax.experimental import pallas as pl
from jax.experimental.pallas import tpu as pltpu
from jax.sharding import PartitionSpec as P

GRID = 96
NB = 2
KPTS = 4
SCREENING = 0.5
RADIUS = GRID // 2 - 1
PENCILS = 16
SLAB = GRID // PENCILS
LANES = 128
ROWS = SLAB * GRID * GRID // LANES
CHUNK = 24

f32 = jnp.float32
bf16 = jnp.bfloat16

KZ = np.array([0] + [s * i for i in range(1, 48) for s in (1, -1)])
KY = np.array([[(8 * j + d // 2) * (1 - 2 * (d % 2)) for d in range(16)] for j in range(6)])
KY[0, 1] = -48
WIDTH = [
    2 * min(RADIUS, int(0.75 + math.sqrt(RADIUS**2 - max(0.0, 8 * j - 0.75) ** 2))) + 1
    for j in range(6)
]
SPLIT4 = LANES - WIDTH[3]
SPLIT5 = LANES - WIDTH[1]
FILL = {
    3: (4, 0, SPLIT4),
    0: (4, SPLIT4, WIDTH[4] - SPLIT4),
    1: (5, 0, SPLIT5),
    2: (5, SPLIT5, WIDTH[5] - SPLIT5),
}
for tile, (band, first, count) in FILL.items():
    assert WIDTH[tile] + count <= LANES


def split(values):
    high = jnp.asarray(values, f32).astype(bf16)
    low = (jnp.asarray(values, f32) - high.astype(f32)).astype(bf16)
    return high, low


def halves(table):
    table = np.asarray(table, np.float32)
    high = table.astype(bf16)
    low = (table - high.astype(np.float32)).astype(bf16)
    return np.stack([high, low])


def angles(rows, cols):
    product = np.outer(rows, cols) % GRID
    angle = product * (2.0 * math.pi / GRID)
    return np.cos(angle), np.sin(angle)


def build_tables():
    cosine, sine = angles(np.arange(GRID), KZ)
    forward_z = np.zeros((2, LANES, 2, LANES))
    inverse_z = np.zeros((2, LANES, 2, LANES))
    n = len(KZ)
    forward_z[0, :GRID, 0, :n] = cosine
    forward_z[1, :GRID, 0, :n] = sine
    forward_z[0, :GRID, 1, :n] = -sine
    forward_z[1, :GRID, 1, :n] = cosine
    inverse_z[0, :n, 0, :GRID] = cosine.T
    inverse_z[1, :n, 0, :GRID] = -sine.T
    inverse_z[0, :n, 1, :GRID] = sine.T
    inverse_z[1, :n, 1, :GRID] = cosine.T
    order_y = np.array([4 * g + j for j in range(4) for g in range(24)])
    cosine, sine = angles(KY.reshape(-1), order_y)
    forward_y = np.block([[cosine, sine], [-sine, cosine]])
    inverse_y = np.block([[cosine.T, -sine.T], [sine.T, cosine.T]])
    freq = np.where(np.arange(GRID) < GRID // 2, np.arange(GRID), np.arange(GRID) - GRID)
    cosine, sine = angles(freq, np.arange(GRID))
    full_f = np.block([[cosine, sine], [-sine, cosine]])
    full_i = np.block([[cosine.T, -sine.T], [sine.T, cosine.T]])
    forward_x = np.zeros((2, 2 * GRID, PENCILS, 16))
    inverse_x = np.zeros((2, PENCILS, 16, 2 * GRID))
    for h in range(2):
        for s in range(PENCILS):
            for c in range(2):
                rows = slice(4 * h + c * SLAB, 4 * h + (c + 1) * SLAB)
                xs = slice(c * GRID + s * SLAB, c * GRID + (s + 1) * SLAB)
                forward_x[h, :, s, rows] = full_f[:, xs]
                inverse_x[h, s, rows, :] = full_i[xs, :]
    lanes = np.zeros((8, 4 * LANES), np.float32)
    lanes[1] = 1000.0
    for tile in range(4):
        base = tile * LANES
        lanes[0, base : base + WIDTH[tile]] = tile
        lanes[1, base : base + WIDTH[tile]] = KZ[: WIDTH[tile]]
        band, first, count = FILL[tile]
        base += WIDTH[tile]
        lanes[0, base : base + count] = band
        lanes[1, base : base + count] = KZ[first : first + count]
    return dict(
        forward_z=halves(forward_z.reshape(2 * LANES, 2 * LANES)),
        inverse_z=halves(inverse_z.reshape(2 * LANES, 2 * LANES)),
        forward_y=halves(forward_y),
        inverse_y=halves(inverse_y),
        forward_x=halves(forward_x.reshape(2, 2 * GRID, 256)),
        inverse_x=halves(inverse_x.reshape(2, 256, 2 * GRID)),
        lanes=lanes,
    )


TABLES = build_tables()


def place():
    kpair = lax.axis_index("kpair")
    band = lax.axis_index("band")
    pencil = lax.axis_index("pencil")
    return kpair, band, pencil


def partner_kpoint(kind, kpair, band):
    core = kpair % 2
    chip = (kpair // 2) * 2 + band
    if kind == "local":
        return (kpair // 2) * 2 + 1 - core
    if kind == "right":
        return ((chip + 1) % 4 // 2) * 2 + core
    if kind == "left":
        return ((chip + 3) % 4 // 2) * 2 + 1 - core
    high = chip // 2
    return (1 - high) * 2 + jnp.where(high == 1, 1 - core, core)


def product3(left_high, left_low, right_high, right_low):
    dot = lambda a, b: jnp.dot(a, b, preferred_element_type=f32)
    return dot(left_high, right_high) + (dot(left_high, right_low) + dot(left_low, right_high))


def lane_index(rows):
    return lax.broadcasted_iota(jnp.int32, (rows, LANES), 1)


def chunk_row(tile, part, x):
    return (tile % 2) * CHUNK + (tile // 2) * 12 + part * SLAB + x


def unpack_kernel(in_ref, out_ref):
    for c in range(2):
        for t in range(72):
            out_ref[pl.ds(c * ROWS + t, SLAB, stride=72), :] = in_ref[c, :, t * LANES : (t + 1) * LANES]


def dense_rows(block):
    return pl.pallas_call(
        unpack_kernel,
        out_shape=jax.ShapeDtypeStruct((2 * ROWS, LANES), f32),
        name="dense_rows",
    )(block)


def finish_kernel(*refs):
    out_ref, total_ref = refs[-2:]
    total = refs[0][...]
    for ref in refs[1:-2]:
        total = total + ref[...]
    total_ref[...] = total
    for c in range(2):
        for t in range(72):
            out_ref[c, :, t * LANES : (t + 1) * LANES] = total_ref[pl.ds(c * ROWS + t, SLAB, stride=72), :]


def finish(*parts):
    return pl.pallas_call(
        finish_kernel,
        out_shape=jax.ShapeDtypeStruct((2, SLAB, GRID * GRID), f32),
        scratch_shapes=[pltpu.VMEM((2 * ROWS, LANES), f32)],
        name="finish",
    )(*parts)


def density_kernel(kinds, where, own_ref, *refs):
    n = len(kinds)
    far_refs = refs[:n]
    z_ref, y_ref, out_ref, dens_ref, high_ref, low_ref = refs[n:]
    kpair, _, _ = where()
    lane = lane_index(24)
    lane16 = lane_index(16)
    for task, kind in enumerate(kinds):
        own_real, own_imag = own_ref[0:ROWS, :], own_ref[ROWS : 2 * ROWS, :]
        far_real, far_imag = far_refs[task][0:ROWS, :], far_refs[task][ROWS : 2 * ROWS, :]
        real = far_real * own_real + far_imag * own_imag
        imag = far_real * own_imag - far_imag * own_real
        if kind == "local":
            packed = kpair % 2 == 1
            real = jnp.where(packed, own_real * own_real + own_imag * own_imag, real)
            imag = jnp.where(packed, far_real * far_real + far_imag * far_imag, imag)
        dens_ref[0:ROWS, :] = real
        dens_ref[ROWS : 2 * ROWS, :] = imag
        for c in range(2):
            cols = slice(c * LANES, (c + 1) * LANES)
            for x in range(SLAB):
                first = c * ROWS + x * 72
                t0, t1, t2 = (dens_ref[pl.ds(first + s, 24, stride=3), :] for s in range(3))
                rows = (
                    t0,
                    jnp.where(lane < 32, pltpu.roll(t0, 32, 1), pltpu.roll(t1, 32, 1)),
                    jnp.where(lane < 64, pltpu.roll(t1, 64, 1), pltpu.roll(t2, 64, 1)),
                    pltpu.roll(t2, 96, 1),
                )
                high, low = split(jnp.concatenate(rows, axis=0))
                high_ref[x * GRID : (x + 1) * GRID, cols] = high
                low_ref[x * GRID : (x + 1) * GRID, cols] = low
        along_z = product3(high_ref[...], low_ref[...], z_ref[0], z_ref[1])
        high, low = split(along_z)
        high_ref[...] = high
        low_ref[...] = low
        for x in range(0, SLAB, 2):
            def columns(ref):
                return jnp.concatenate(
                    [
                        jnp.concatenate(
                            [ref[v * GRID : (v + 1) * GRID, 0:LANES], ref[v * GRID : (v + 1) * GRID, LANES:]],
                            axis=0,
                        )
                        for v in (x, x + 1)
                    ],
                    axis=1,
                )
            along_y = product3(y_ref[0], y_ref[1], columns(high_ref), columns(low_ref))
            for v in range(2):
                for c in range(2):
                    bands = [
                        along_y[c * GRID + 16 * j : c * GRID + 16 * j + 16, v * LANES : (v + 1) * LANES]
                        for j in range(6)
                    ]
                    for tile in range(4):
                        band, start, _ = FILL[tile]
                        shift = (WIDTH[tile] - start) % LANES
                        value = jnp.where(lane16 < WIDTH[tile], bands[tile], pltpu.roll(bands[band], shift, 1))
                        row = task * 2 * CHUNK + chunk_row(tile, c, x + v)
                        out_ref[pl.ds(row, 16, stride=n * 2 * CHUNK), :] = value


def densities(kinds, own, fars, where=place, interpret=False):
    n = len(kinds)
    out = pl.pallas_call(
        lambda *refs: density_kernel(kinds, where, *refs),
        out_shape=jax.ShapeDtypeStruct((PENCILS * n * 2 * CHUNK, LANES), f32),
        scratch_shapes=[
            pltpu.VMEM((2 * ROWS, LANES), f32),
            pltpu.VMEM((SLAB * GRID, 2 * LANES), bf16),
            pltpu.VMEM((SLAB * GRID, 2 * LANES), bf16),
        ],
        name="densities_" + "_".join(kinds),
        interpret=interpret,
    )(own, *fars, TABLES["forward_z"], TABLES["forward_y"])
    return out.reshape(PENCILS, n, 2, CHUNK, LANES)


def filter_kernel(kinds, where, coords_ref, in_ref, forward_ref, inverse_ref, lanes_ref, out_ref):
    kpair, band, pencil = where()
    own = [coords_ref[kpair, a] for a in range(3)]
    factor = (2.0 * math.pi / GRID) ** 2
    scale = -1.0 / (KPTS * NB) / GRID**3
    slot = lanes_ref[0:1, :]
    sign = (1 - 2 * (pencil % 2)).astype(f32)
    ky = sign * (8.0 * slot + (pencil // 2).astype(f32))
    ky = jnp.where(slot == jnp.where(pencil == 1, 0.0, -1.0), -48.0, ky)
    kz = lanes_ref[1:2, :]
    index = lax.broadcasted_iota(jnp.int32, (GRID, 2 * LANES), 0)
    kx = jnp.where(index < GRID // 2, index, index - GRID).astype(f32)
    for task, kind in enumerate(kinds):
        partner = partner_kpoint(kind, kpair, band)
        shift = [(own[a] - coords_ref[partner, a]).astype(f32) * 0.25 for a in range(3)]
        if kind == "local":
            shift = [jnp.where(kpair % 2 == 1, 0.0, d) for d in shift]
        plane = (ky + shift[1]) ** 2 + (kz + shift[2]) ** 2
        along_x = (kx + shift[0]) ** 2
        previous = None
        for h in range(2):
            rows = [
                in_ref[:, task, l, 8 * h : 8 * h + 16, :].reshape(256, LANES) for l in range(2)
            ]
            high, low = split(jnp.concatenate(rows, axis=1))
            spectrum = product3(forward_ref[0, h], forward_ref[1, h], high, low)
            squared = along_x + plane[:, h * 256 : (h + 1) * 256]
            coulomb = jnp.where(
                squared <= RADIUS * RADIUS, 4.0 * math.pi / (factor * squared + SCREENING), 0.0
            ) * scale
            spectrum = jnp.concatenate([spectrum[:GRID] * coulomb, spectrum[GRID:] * coulomb], axis=0)
            high, low = split(spectrum)
            back = product3(inverse_ref[0, h], inverse_ref[1, h], high, low).reshape(PENCILS, 16, 2 * LANES)
            for l in range(2):
                part = back[:, :, l * LANES : (l + 1) * LANES]
                if h == 0:
                    out_ref[:, task, l, 0:8, :] = part[:, 0:8]
                else:
                    out_ref[:, task, l, 16:24, :] = part[:, 8:16]
                    out_ref[:, task, l, 8:16, :] = part[:, 0:8] + previous[:, 8:16, l * LANES : (l + 1) * LANES]
            previous = back


def filtered(kinds, coords, chunks, where=place, interpret=False):
    vmem = pl.BlockSpec(memory_space=pltpu.VMEM)
    return pl.pallas_call(
        lambda *refs: filter_kernel(kinds, where, *refs),
        out_shape=jax.ShapeDtypeStruct(chunks.shape, f32),
        in_specs=[pl.BlockSpec(memory_space=pltpu.SMEM), vmem, vmem, vmem, vmem],
        out_specs=vmem,
        name="filtered_" + "_".join(kinds),
        interpret=interpret,
    )(coords, chunks, TABLES["forward_x"], TABLES["inverse_x"], TABLES["lanes"])


def potential_kernel(kinds, where, first, in_ref, own_ref, *refs):
    n = len(kinds)
    far_refs = refs[:n]
    refs = refs[n:]
    if not first:
        base_ref, refs = refs[0], refs[1:]
    z_ref, y_ref, sum_ref = refs[:3]
    back_refs = refs[3 : 3 + n]
    pot_ref, high_ref, low_ref = refs[3 + n :]
    kpair, _, _ = where()
    lane = lane_index(24)
    lane16 = lane_index(16)
    for task, kind in enumerate(kinds):
        for x in range(0, SLAB, 2):
            pair = []
            for v in (x, x + 1):
                parts = []
                for c in range(2):
                    tiles = [
                        in_ref[pl.ds(task * 2 * CHUNK + chunk_row(t, c, v), 16, stride=n * 2 * CHUNK), :]
                        for t in range(4)
                    ]
                    bands = [jnp.where(lane16 < WIDTH[t], tiles[t], 0.0) for t in range(4)]
                    for band, (ta, tb) in ((4, (3, 0)), (5, (1, 2))):
                        _, sa, ca = FILL[ta]
                        _, sb, cb = FILL[tb]
                        a = pltpu.roll(tiles[ta], (sa - WIDTH[ta]) % LANES, 1)
                        b = pltpu.roll(tiles[tb], (sb - WIDTH[tb]) % LANES, 1)
                        bands.append(jnp.where(lane16 < ca, a, jnp.where(lane16 < ca + cb, b, 0.0)))
                    parts += bands
                pair.append(jnp.concatenate(parts, axis=0))
            high, low = split(jnp.concatenate(pair, axis=1))
            along_y = product3(y_ref[0], y_ref[1], high, low)
            high, low = split(along_y)
            for v in range(2):
                for c in range(2):
                    rows = slice((x + v) * GRID, (x + v + 1) * GRID)
                    cols = slice(c * LANES, (c + 1) * LANES)
                    high_ref[rows, cols] = high[c * GRID : (c + 1) * GRID, v * LANES : (v + 1) * LANES]
                    low_ref[rows, cols] = low[c * GRID : (c + 1) * GRID, v * LANES : (v + 1) * LANES]
        along_z = product3(high_ref[...], low_ref[...], z_ref[0], z_ref[1])
        for c in range(2):
            for x in range(SLAB):
                v0, v1, v2, v3 = (
                    along_z[x * GRID + 24 * j : x * GRID + 24 * j + 24, c * LANES : (c + 1) * LANES]
                    for j in range(4)
                )
                v1, v2, v3 = pltpu.roll(v1, 96, 1), pltpu.roll(v2, 64, 1), pltpu.roll(v3, 32, 1)
                rows = (jnp.where(lane < 96, v0, v1), jnp.where(lane < 64, v1, v2), jnp.where(lane < 32, v2, v3))
                for s in range(3):
                    pot_ref[pl.ds(c * ROWS + x * 72 + s, 24, stride=3), :] = rows[s]
        own_real, own_imag = own_ref[0:ROWS, :], own_ref[ROWS : 2 * ROWS, :]
        far_real, far_imag = far_refs[task][0:ROWS, :], far_refs[task][ROWS : 2 * ROWS, :]
        pot_real, pot_imag = pot_ref[0:ROWS, :], pot_ref[ROWS : 2 * ROWS, :]
        here_real = far_real * pot_real - far_imag * pot_imag
        here_imag = far_real * pot_imag + far_imag * pot_real
        there_real = own_real * pot_real + own_imag * pot_imag
        there_imag = own_imag * pot_real - own_real * pot_imag
        if kind == "local":
            packed = kpair % 2 == 1
            here_real = jnp.where(packed, own_real * pot_real, here_real)
            here_imag = jnp.where(packed, own_imag * pot_real, here_imag)
            there_real = jnp.where(packed, far_real * pot_imag, there_real)
            there_imag = jnp.where(packed, far_imag * pot_imag, there_imag)
        if task > 0:
            here_real = here_real + sum_ref[0:ROWS, :]
            here_imag = here_imag + sum_ref[ROWS : 2 * ROWS, :]
        elif not first:
            here_real = here_real + base_ref[0:ROWS, :]
            here_imag = here_imag + base_ref[ROWS : 2 * ROWS, :]
        sum_ref[0:ROWS, :] = here_real
        sum_ref[ROWS : 2 * ROWS, :] = here_imag
        back_refs[task][0:ROWS, :] = there_real
        back_refs[task][ROWS : 2 * ROWS, :] = there_imag


def potentials(kinds, chunks, own, fars, base=None, where=place, interpret=False):
    n = len(kinds)
    dense = jax.ShapeDtypeStruct((2 * ROWS, LANES), f32)
    bases = () if base is None else (base,)
    out = pl.pallas_call(
        lambda *refs: potential_kernel(kinds, where, base is None, *refs),
        out_shape=[dense] * (n + 1),
        scratch_shapes=[
            pltpu.VMEM((2 * ROWS, LANES), f32),
            pltpu.VMEM((SLAB * GRID, 2 * LANES), bf16),
            pltpu.VMEM((SLAB * GRID, 2 * LANES), bf16),
        ],
        name="potentials_" + "_".join(kinds),
        interpret=interpret,
    )(
        chunks.reshape(PENCILS * n * 2 * CHUNK, LANES),
        own,
        *fars,
        *bases,
        TABLES["inverse_z"],
        TABLES["inverse_y"],
    )
    return out[0], out[1:]


def line(chip, core):
    chip %= 4
    return (chip // 2) * 4 + core * 2 + chip % 2


def route(kind):
    pairs = []
    for chip in range(4):
        for core in range(2):
            if kind == "local":
                source = line(chip, 1 - core)
            elif kind == "right":
                source = line(chip + 1, core)
            elif kind == "left":
                source = line(chip - 1, 1 - core)
            else:
                source = line(chip + 2, core if chip < 2 else 1 - core)
            pairs.append((source, line(chip, core)))
    return pairs


def fetch(kind, block):
    return lax.ppermute(block, ("kpair", "band"), route(kind))


def give_back(kind, block):
    return lax.ppermute(block, ("kpair", "band"), [(b, a) for a, b in route(kind)])


def transpose(chunks):
    return lax.all_to_all(chunks, "pencil", 0, 0, tiled=True)


BATCHES = (("local",), ("across",), ("right", "left"))
RETURNS = (1, 2, 0)


def body(orbitals, kcoords):
    own = dense_rows(orbitals.reshape(2, SLAB, GRID * GRID))
    far = {kind: fetch(kind, own) for kind in ("local", "across", "right", "left")}
    sent = []
    for kinds in BATCHES:
        fars = [far[kind] for kind in kinds]
        sent.append(transpose(densities(kinds, own, fars)))
    spectra = {}
    total = None
    returned = []
    for index in RETURNS:
        kinds = BATCHES[index]
        spectra[index] = transpose(filtered(kinds, kcoords, sent[index]))
    for index in RETURNS:
        kinds = BATCHES[index]
        total, back = potentials(kinds, spectra[index], own, [far[kind] for kind in kinds], total)
        returned += [give_back(kind, block) for kind, block in zip(kinds, back)]
    out = finish(total, *returned)
    return out.reshape(2, 1, 1, SLAB, GRID * GRID)


def solution(mesh):
    in_specs = (P(None, "kpair", "band", "pencil", None), P())
    out_specs = P(None, "kpair", "band", "pencil", None)
    return jax.shard_map(body, mesh=mesh, in_specs=in_specs, out_specs=out_specs, check_vma=False)
```

```python
import math

import jax
import jax.numpy as jnp
import numpy as np
from jax import lax
from jax.experimental import pallas as pl
from jax.experimental.pallas import tpu as pltpu
from jax.sharding import PartitionSpec as P

GRID = 96
NB = 2
KPTS = 4
SCREENING = 0.5
RADIUS = GRID // 2 - 1
PENCILS = 16
SLAB = GRID // PENCILS
LANES = 128
ROWS = SLAB * GRID * GRID // LANES
CHUNK = 24

f32 = jnp.float32
bf16 = jnp.bfloat16

KZ = np.array([0] + [s * i for i in range(1, 48) for s in (1, -1)])
KY = np.array([[(8 * j + d // 2) * (1 - 2 * (d % 2)) for d in range(16)] for j in range(6)])
KY[0, 1] = -48
WIDTH = [
    2 * min(RADIUS, int(0.75 + math.sqrt(RADIUS**2 - max(0.0, 8 * j - 0.75) ** 2))) + 1
    for j in range(6)
]
SPLIT4 = LANES - WIDTH[3]
SPLIT5 = LANES - WIDTH[1]
FILL = {
    3: (4, 0, SPLIT4),
    0: (4, SPLIT4, WIDTH[4] - SPLIT4),
    1: (5, 0, SPLIT5),
    2: (5, SPLIT5, WIDTH[5] - SPLIT5),
}
for tile, (band, first, count) in FILL.items():
    assert WIDTH[tile] + count <= LANES


def split(values):
    high = jnp.asarray(values, f32).astype(bf16)
    low = (jnp.asarray(values, f32) - high.astype(f32)).astype(bf16)
    return high, low


def halves(table):
    table = np.asarray(table, np.float32)
    high = table.astype(bf16)
    low = (table - high.astype(np.float32)).astype(bf16)
    return np.stack([high, low])


def angles(rows, cols):
    product = np.outer(rows, cols) % GRID
    angle = product * (2.0 * math.pi / GRID)
    return np.cos(angle), np.sin(angle)


def build_tables():
    cosine, sine = angles(np.arange(GRID), KZ)
    forward_z = np.zeros((2, LANES, 2, LANES))
    inverse_z = np.zeros((2, LANES, 2, LANES))
    n = len(KZ)
    forward_z[0, :GRID, 0, :n] = cosine
    forward_z[1, :GRID, 0, :n] = sine
    forward_z[0, :GRID, 1, :n] = -sine
    forward_z[1, :GRID, 1, :n] = cosine
    inverse_z[0, :n, 0, :GRID] = cosine.T
    inverse_z[1, :n, 0, :GRID] = -sine.T
    inverse_z[0, :n, 1, :GRID] = sine.T
    inverse_z[1, :n, 1, :GRID] = cosine.T
    order_y = np.array([4 * g + j for j in range(4) for g in range(24)])
    cosine, sine = angles(KY.reshape(-1), order_y)
    forward_y = np.block([[cosine, sine], [-sine, cosine]])
    inverse_y = np.block([[cosine.T, -sine.T], [sine.T, cosine.T]])
    freq = np.where(np.arange(GRID) < GRID // 2, np.arange(GRID), np.arange(GRID) - GRID)
    cosine, sine = angles(freq, np.arange(GRID))
    full_f = np.block([[cosine, sine], [-sine, cosine]])
    full_i = np.block([[cosine.T, -sine.T], [sine.T, cosine.T]])
    forward_x = np.zeros((2, 2 * GRID, PENCILS, 16))
    inverse_x = np.zeros((2, PENCILS, 16, 2 * GRID))
    for h in range(2):
        for s in range(PENCILS):
            for c in range(2):
                rows = slice(4 * h + c * SLAB, 4 * h + (c + 1) * SLAB)
                xs = slice(c * GRID + s * SLAB, c * GRID + (s + 1) * SLAB)
                forward_x[h, :, s, rows] = full_f[:, xs]
                inverse_x[h, s, rows, :] = full_i[xs, :]
    lanes = np.zeros((8, 4 * LANES), np.float32)
    lanes[1] = 1000.0
    for tile in range(4):
        base = tile * LANES
        lanes[0, base : base + WIDTH[tile]] = tile
        lanes[1, base : base + WIDTH[tile]] = KZ[: WIDTH[tile]]
        band, first, count = FILL[tile]
        base += WIDTH[tile]
        lanes[0, base : base + count] = band
        lanes[1, base : base + count] = KZ[first : first + count]
    return dict(
        forward_z=halves(forward_z.reshape(2 * LANES, 2 * LANES)),
        inverse_z=halves(inverse_z.reshape(2 * LANES, 2 * LANES)),
        forward_y=halves(forward_y),
        inverse_y=halves(inverse_y),
        forward_x=halves(forward_x.reshape(2, 2 * GRID, 256)),
        inverse_x=halves(inverse_x.reshape(2, 256, 2 * GRID)),
        lanes=lanes,
    )


TABLES = build_tables()


def place():
    kpair = lax.axis_index("kpair")
    band = lax.axis_index("band")
    pencil = lax.axis_index("pencil")
    return kpair, band, pencil


def partners(kpair, band):
    core = kpair % 2
    chip = (kpair // 2) * 2 + band
    right_core = jnp.where(chip == 0, 1 - core, core)
    left_core = jnp.where(chip == 1, core, 1 - core)
    right = ((chip + 1) % 4 // 2) * 2 + right_core
    left = ((chip + 3) % 4 // 2) * 2 + left_core
    return right, left


def product3(left_high, left_low, right_high, right_low):
    dot = lambda a, b: jnp.dot(a, b, preferred_element_type=f32)
    return dot(left_high, right_high) + (dot(left_high, right_low) + dot(left_low, right_high))


def lane_index(rows):
    return lax.broadcasted_iota(jnp.int32, (rows, LANES), 1)


def chunk_row(tile, part, x):
    return (tile % 2) * CHUNK + (tile // 2) * 12 + part * SLAB + x


VMEM_LIMIT = 12 * 1024 * 1024


SPACE = {"vmem": pltpu.VMEM, "hbm": pltpu.HBM}


def kept_in(place, array):
    return pltpu.with_memory_space_constraint(array, SPACE[place]) if place in SPACE else array


class Fetched:
    def __init__(self, source, target, semaphore):
        self.target = target
        self.copy = pltpu.make_async_copy(source, target, semaphore)
        self.copy.start()
        self.pending = True

    def get(self):
        if self.pending:
            self.copy.wait()
            self.pending = False
        return self.target


class Ready:
    def __init__(self, ref):
        self.ref = ref

    def get(self):
        return self.ref


def call(kernel, out_shapes, scratch, args, interpret=False):
    places = [place for place, _ in args]
    arrays = [jnp.asarray(array) for _, array in args]
    specs = {
        "smem": pl.BlockSpec(memory_space=pltpu.SMEM),
        "vmem": pl.BlockSpec(memory_space=pltpu.VMEM),
        "hbm": pl.BlockSpec(memory_space=pltpu.HBM),
    }
    remote = [array for place, array in zip(places, arrays) if place == "hbm"]
    n_in, n_out = len(args), len(out_shapes)

    def entry(*refs):
        inputs, outputs = refs[:n_in], refs[n_in : n_in + n_out]
        rest = refs[n_in + n_out :]
        targets, semaphores, own_scratch = rest[: len(remote)], rest[len(remote)], rest[len(remote) + 1 :]
        handles, k = [], 0
        for place, ref in zip(places, inputs):
            if place == "hbm":
                handles.append(Fetched(ref, targets[k], semaphores.at[k]))
                k += 1
            else:
                handles.append(Ready(ref))
        kernel(*handles, *outputs, *own_scratch)

    return pl.pallas_call(
        entry,
        out_shape=out_shapes,
        in_specs=[specs[place] for place in places],
        out_specs=[specs["vmem"]] * n_out,
        scratch_shapes=[pltpu.VMEM(array.shape, array.dtype) for array in remote]
        + [pltpu.SemaphoreType.DMA((max(1, len(remote)),))]
        + scratch,
        interpret=interpret,
        compiler_params=pltpu.CompilerParams(vmem_limit_bytes=VMEM_LIMIT),
    )(*(kept_in(place, array) for place, array in zip(places, arrays)))


LOCAL = (("local", 0, 1),)
REMOTE = (("across", 1, 2), ("right", 0, 1), ("left", 0, 2))


def density_kernel(tasks, members, where, *refs):
    n = len(tasks)
    orbitals = refs[:members]
    z_table, y_table, out_ref, dens_ref, high_ref, low_ref = refs[members:]
    kpair, _, _ = where()
    lane = lane_index(24)
    lane16 = lane_index(16)
    for task, (kind, a, b) in enumerate(tasks):
        own_ref, far_ref = orbitals[a].get(), orbitals[b].get()
        own_real, own_imag = own_ref[0:ROWS, :], own_ref[ROWS : 2 * ROWS, :]
        far_real, far_imag = far_ref[0:ROWS, :], far_ref[ROWS : 2 * ROWS, :]
        real = far_real * own_real + far_imag * own_imag
        imag = far_real * own_imag - far_imag * own_real
        if kind == "local":
            packed = kpair % 2 == 1
            real = jnp.where(packed, own_real * own_real + own_imag * own_imag, real)
            imag = jnp.where(packed, far_real * far_real + far_imag * far_imag, imag)
        dens_ref[0:ROWS, :] = real
        dens_ref[ROWS : 2 * ROWS, :] = imag
        for c in range(2):
            cols = slice(c * LANES, (c + 1) * LANES)
            for x in range(SLAB):
                first = c * ROWS + x * 72
                t0, t1, t2 = (dens_ref[pl.ds(first + s, 24, stride=3), :] for s in range(3))
                rows = (
                    t0,
                    jnp.where(lane < 32, pltpu.roll(t0, 32, 1), pltpu.roll(t1, 32, 1)),
                    jnp.where(lane < 64, pltpu.roll(t1, 64, 1), pltpu.roll(t2, 64, 1)),
                    pltpu.roll(t2, 96, 1),
                )
                high, low = split(jnp.concatenate(rows, axis=0))
                high_ref[x * GRID : (x + 1) * GRID, cols] = high
                low_ref[x * GRID : (x + 1) * GRID, cols] = low
        z_ref = z_table.get()
        along_z = product3(high_ref[...], low_ref[...], z_ref[0], z_ref[1])
        high, low = split(along_z)
        high_ref[...] = high
        low_ref[...] = low
        y_ref = y_table.get()
        for x in range(0, SLAB, 2):
            def columns(ref):
                return jnp.concatenate(
                    [
                        jnp.concatenate(
                            [ref[v * GRID : (v + 1) * GRID, 0:LANES], ref[v * GRID : (v + 1) * GRID, LANES:]],
                            axis=0,
                        )
                        for v in (x, x + 1)
                    ],
                    axis=1,
                )

            along_y = product3(y_ref[0], y_ref[1], columns(high_ref), columns(low_ref))
            for v in range(2):
                for c in range(2):
                    bands = [
                        along_y[c * GRID + 16 * j : c * GRID + 16 * j + 16, v * LANES : (v + 1) * LANES]
                        for j in range(6)
                    ]
                    for tile in range(4):
                        band, start, _ = FILL[tile]
                        shift = (WIDTH[tile] - start) % LANES
                        value = jnp.where(lane16 < WIDTH[tile], bands[tile], pltpu.roll(bands[band], shift, 1))
                        row = task * 2 * CHUNK + chunk_row(tile, c, x + v)
                        out_ref[pl.ds(row, 16, stride=n * 2 * CHUNK), :] = value


def scratch_fields():
    return [
        pltpu.VMEM((2 * ROWS, LANES), f32),
        pltpu.VMEM((SLAB * GRID, 2 * LANES), bf16),
        pltpu.VMEM((SLAB * GRID, 2 * LANES), bf16),
    ]


def densities(tasks, orbitals, where=place, interpret=False):
    n = len(tasks)
    (out,) = call(
        lambda *refs: density_kernel(tasks, len(orbitals), where, *refs),
        [pltpu.HBM((PENCILS * n * 2 * CHUNK, LANES), f32)],
        scratch_fields(),
        [*orbitals, ("hbm", TABLES["forward_z"]), ("hbm", TABLES["forward_y"])],
        interpret,
    )
    return out.reshape(PENCILS, n, 2, CHUNK, LANES)


def filter_kernel(tasks, where, coords, chunks, lanes, forward_table, inverse_table, out_ref):
    coords_ref, in_ref, lanes_ref = coords.get(), chunks.get(), lanes.get()
    kpair, band, pencil = where()
    right, left = partners(kpair, band)
    points = {
        "local": (kpair, jnp.where(kpair % 2 == 1, kpair, kpair + 1)),
        "right": (kpair, right),
        "left": (kpair, left),
        "across": (right, left),
    }
    factor = (2.0 * math.pi / GRID) ** 2
    scale = -1.0 / (KPTS * NB) / GRID**3
    slot = lanes_ref[0:1, :]
    sign = (1 - 2 * (pencil % 2)).astype(f32)
    ky = sign * (8.0 * slot + (pencil // 2).astype(f32))
    ky = jnp.where(slot == jnp.where(pencil == 1, 0.0, -1.0), -48.0, ky)
    kz = lanes_ref[1:2, :]
    index = lax.broadcasted_iota(jnp.int32, (GRID, 2 * LANES), 0)
    kx = jnp.where(index < GRID // 2, index, index - GRID).astype(f32)
    for task, (kind, _, _) in enumerate(tasks):
        here, there = points[kind]
        shift = [(coords_ref[here, a] - coords_ref[there, a]).astype(f32) * 0.25 for a in range(3)]
        plane = (ky + shift[1]) ** 2 + (kz + shift[2]) ** 2
        along_x = (kx + shift[0]) ** 2
        previous = None
        for h in range(2):
            rows = [
                in_ref[:, task, l, 8 * h : 8 * h + 16, :].reshape(256, LANES) for l in range(2)
            ]
            high, low = split(jnp.concatenate(rows, axis=1))
            forward_ref = forward_table.get()
            spectrum = product3(forward_ref[0, h], forward_ref[1, h], high, low)
            squared = along_x + plane[:, h * 256 : (h + 1) * 256]
            coulomb = jnp.where(
                squared <= RADIUS * RADIUS, 4.0 * math.pi / (factor * squared + SCREENING), 0.0
            ) * scale
            spectrum = jnp.concatenate([spectrum[:GRID] * coulomb, spectrum[GRID:] * coulomb], axis=0)
            high, low = split(spectrum)
            inverse_ref = inverse_table.get()
            back = product3(inverse_ref[0, h], inverse_ref[1, h], high, low).reshape(PENCILS, 16, 2 * LANES)
            for l in range(2):
                part = back[:, :, l * LANES : (l + 1) * LANES]
                if h == 0:
                    out_ref[:, task, l, 0:8, :] = part[:, 0:8]
                else:
                    out_ref[:, task, l, 16:24, :] = part[:, 8:16]
                    out_ref[:, task, l, 8:16, :] = part[:, 0:8] + previous[:, 8:16, l * LANES : (l + 1) * LANES]
            previous = back


def filtered(tasks, coords, chunks, source, where=place, interpret=False):
    (out,) = call(
        lambda *refs: filter_kernel(tasks, where, *refs),
        [pltpu.HBM(chunks.shape, f32)],
        [],
        [
            ("smem", coords),
            (source, chunks),
            ("hbm", TABLES["lanes"]),
            ("hbm", TABLES["forward_x"]),
            ("hbm", TABLES["inverse_x"]),
        ],
        interpret,
    )
    return out


def potential_kernel(tasks, members, where, chunks, *refs):
    n = len(tasks)
    in_ref = chunks.get()
    orbitals = refs[:members]
    y_table, z_table = refs[members : members + 2]
    sum_refs = refs[members + 2 : 2 * members + 2]
    pot_ref, high_ref, low_ref = refs[2 * members + 2 :]
    touched = set()
    kpair, _, _ = where()
    lane = lane_index(24)
    lane16 = lane_index(16)
    for task, (kind, a, b) in enumerate(tasks):
        for x in range(0, SLAB, 2):
            pair = []
            for v in (x, x + 1):
                parts = []
                for c in range(2):
                    tiles = [
                        in_ref[pl.ds(task * 2 * CHUNK + chunk_row(t, c, v), 16, stride=n * 2 * CHUNK), :]
                        for t in range(4)
                    ]
                    bands = [jnp.where(lane16 < WIDTH[t], tiles[t], 0.0) for t in range(4)]
                    for (ta, tb) in ((3, 0), (1, 2)):
                        _, sa, ca = FILL[ta]
                        _, sb, cb = FILL[tb]
                        head = pltpu.roll(tiles[ta], (sa - WIDTH[ta]) % LANES, 1)
                        tail = pltpu.roll(tiles[tb], (sb - WIDTH[tb]) % LANES, 1)
                        bands.append(jnp.where(lane16 < ca, head, jnp.where(lane16 < ca + cb, tail, 0.0)))
                    parts += bands
                pair.append(jnp.concatenate(parts, axis=0))
            high, low = split(jnp.concatenate(pair, axis=1))
            y_ref = y_table.get()
            along_y = product3(y_ref[0], y_ref[1], high, low)
            high, low = split(along_y)
            for v in range(2):
                for c in range(2):
                    rows = slice((x + v) * GRID, (x + v + 1) * GRID)
                    cols = slice(c * LANES, (c + 1) * LANES)
                    high_ref[rows, cols] = high[c * GRID : (c + 1) * GRID, v * LANES : (v + 1) * LANES]
                    low_ref[rows, cols] = low[c * GRID : (c + 1) * GRID, v * LANES : (v + 1) * LANES]
        z_ref = z_table.get()
        along_z = product3(high_ref[...], low_ref[...], z_ref[0], z_ref[1])
        for c in range(2):
            for x in range(SLAB):
                v0, v1, v2, v3 = (
                    along_z[x * GRID + 24 * j : x * GRID + 24 * j + 24, c * LANES : (c + 1) * LANES]
                    for j in range(4)
                )
                v1, v2, v3 = pltpu.roll(v1, 96, 1), pltpu.roll(v2, 64, 1), pltpu.roll(v3, 32, 1)
                rows = (jnp.where(lane < 96, v0, v1), jnp.where(lane < 64, v1, v2), jnp.where(lane < 32, v2, v3))
                for s in range(3):
                    pot_ref[pl.ds(c * ROWS + x * 72 + s, 24, stride=3), :] = rows[s]
        own_ref, far_ref = orbitals[a].get(), orbitals[b].get()
        own_real, own_imag = own_ref[0:ROWS, :], own_ref[ROWS : 2 * ROWS, :]
        far_real, far_imag = far_ref[0:ROWS, :], far_ref[ROWS : 2 * ROWS, :]
        pot_real, pot_imag = pot_ref[0:ROWS, :], pot_ref[ROWS : 2 * ROWS, :]
        here_real = far_real * pot_real - far_imag * pot_imag
        here_imag = far_real * pot_imag + far_imag * pot_real
        there_real = own_real * pot_real + own_imag * pot_imag
        there_imag = own_imag * pot_real - own_real * pot_imag
        if kind == "local":
            packed = kpair % 2 == 1
            here_real = jnp.where(packed, own_real * pot_real, here_real)
            here_imag = jnp.where(packed, own_imag * pot_real, here_imag)
            there_real = jnp.where(packed, far_real * pot_imag, there_real)
            there_imag = jnp.where(packed, far_imag * pot_imag, there_imag)
        for member, real, imag in ((a, here_real, here_imag), (b, there_real, there_imag)):
            if member in touched:
                real = real + sum_refs[member][0:ROWS, :]
                imag = imag + sum_refs[member][ROWS : 2 * ROWS, :]
            touched.add(member)
            sum_refs[member][0:ROWS, :] = real
            sum_refs[member][ROWS : 2 * ROWS, :] = imag


def potentials(tasks, chunks, orbitals, where=place, interpret=False):
    n = len(tasks)
    return call(
        lambda *refs: potential_kernel(tasks, len(orbitals), where, *refs),
        [pltpu.HBM((2 * ROWS, LANES), f32)] * len(orbitals),
        scratch_fields(),
        [
            ("vmem", chunks.reshape(PENCILS * n * 2 * CHUNK, LANES)),
            *orbitals,
            ("hbm", TABLES["inverse_y"]),
            ("hbm", TABLES["inverse_z"]),
        ],
        interpret,
    )


def line(chip, core):
    chip %= 4
    return (chip // 2) * 4 + core * 2 + chip % 2


TURN = (1, 0, 0, 0)


def route(kind):
    pairs = []
    for chip in range(4):
        for core in range(2):
            if kind == "local":
                source = line(chip, 1 - core)
            elif kind == "right":
                source = line(chip + 1, core ^ TURN[chip])
            else:
                source = line(chip - 1, core ^ (1 - TURN[chip - 1]))
            pairs.append((source, line(chip, core)))
    return pairs


def fetch(kind, block):
    return lax.ppermute(block, ("kpair", "band"), route(kind))


def give_back(kind, block):
    return lax.ppermute(block, ("kpair", "band"), [(b, a) for a, b in route(kind)])


def transpose(chunks):
    return lax.all_to_all(chunks, "pencil", 0, 0, tiled=True)


def body(orbitals, kcoords):
    own = orbitals.reshape(2 * ROWS, LANES)
    right, left, other = fetch("right", own), fetch("left", own), fetch("local", own)
    near = [("hbm", own), ("vmem", other)]
    far = [("hbm", own), ("vmem", right), ("vmem", left)]
    chunks_near = densities(LOCAL, near)
    sent_near = transpose(chunks_near)
    chunks_far = densities(REMOTE, far)
    sent_far = transpose(chunks_far)
    spectrum_near = filtered(LOCAL, kcoords, sent_near, "hbm")
    spectrum_far = filtered(REMOTE, kcoords, sent_far, "vmem")
    back_far = transpose(spectrum_far)
    back_far, spectrum_near = lax.optimization_barrier((back_far, spectrum_near))
    back_near = transpose(spectrum_near)
    far_sum, for_right, for_left = potentials(REMOTE, back_far, far)
    from_right, from_left = give_back("right", for_right), give_back("left", for_left)
    near_sum, for_other = potentials(LOCAL, back_near, near)
    from_other = give_back("local", for_other)
    out = (far_sum + near_sum) + from_other + (from_right + from_left)
    return out.reshape(2, 1, 1, SLAB, GRID * GRID)


def solution(mesh):
    in_specs = (P(None, "kpair", "band", "pencil", None), P())
    out_specs = P(None, "kpair", "band", "pencil", None)
    return jax.shard_map(body, mesh=mesh, in_specs=in_specs, out_specs=out_specs, check_vma=False)
```

```python
import math

import jax
import jax.numpy as jnp
import numpy as np
from jax import lax
from jax.experimental import pallas as pl
from jax.experimental.pallas import tpu as pltpu
from jax.sharding import PartitionSpec as P

GRID = 96
NB = 2
KPTS = 4
SCREENING = 0.5
RADIUS = GRID // 2 - 1
PENCILS = 16
SLAB = GRID // PENCILS
LANES = 128
ROWS = SLAB * GRID * GRID // LANES
CHUNK = 24

f32 = jnp.float32
bf16 = jnp.bfloat16

KZ = np.array([0] + [s * i for i in range(1, 48) for s in (1, -1)])
KY = np.array([[(8 * j + d // 2) * (1 - 2 * (d % 2)) for d in range(16)] for j in range(6)])
KY[0, 1] = -48
WIDTH = [
    2 * min(RADIUS, int(0.75 + math.sqrt(RADIUS**2 - max(0.0, 8 * j - 0.75) ** 2))) + 1
    for j in range(6)
]
SPLIT4 = LANES - WIDTH[3]
SPLIT5 = LANES - WIDTH[1]
FILL = {
    3: (4, 0, SPLIT4),
    0: (4, SPLIT4, WIDTH[4] - SPLIT4),
    1: (5, 0, SPLIT5),
    2: (5, SPLIT5, WIDTH[5] - SPLIT5),
}
for tile, (band, first, count) in FILL.items():
    assert WIDTH[tile] + count <= LANES


def split(values):
    high = jnp.asarray(values, f32).astype(bf16)
    low = (jnp.asarray(values, f32) - high.astype(f32)).astype(bf16)
    return high, low


def halves(table):
    table = np.asarray(table, np.float32)
    high = table.astype(bf16)
    low = (table - high.astype(np.float32)).astype(bf16)
    return np.stack([high, low])


def angles(rows, cols):
    product = np.outer(rows, cols) % GRID
    angle = product * (2.0 * math.pi / GRID)
    return np.cos(angle), np.sin(angle)


def build_tables():
    cosine, sine = angles(np.arange(GRID), KZ)
    forward_z = np.zeros((2, LANES, 2, LANES))
    inverse_z = np.zeros((2, LANES, 2, LANES))
    n = len(KZ)
    forward_z[0, :GRID, 0, :n] = cosine
    forward_z[1, :GRID, 0, :n] = sine
    forward_z[0, :GRID, 1, :n] = -sine
    forward_z[1, :GRID, 1, :n] = cosine
    inverse_z[0, :n, 0, :GRID] = cosine.T
    inverse_z[1, :n, 0, :GRID] = -sine.T
    inverse_z[0, :n, 1, :GRID] = sine.T
    inverse_z[1, :n, 1, :GRID] = cosine.T
    order_y = np.array([4 * g + j for j in range(4) for g in range(24)])
    cosine, sine = angles(KY.reshape(-1), order_y)
    forward_y = np.block([[cosine, sine], [-sine, cosine]])
    inverse_y = np.block([[cosine.T, -sine.T], [sine.T, cosine.T]])
    freq = np.where(np.arange(GRID) < GRID // 2, np.arange(GRID), np.arange(GRID) - GRID)
    cosine, sine = angles(freq, np.arange(GRID))
    full_f = np.block([[cosine, sine], [-sine, cosine]])
    full_i = np.block([[cosine.T, -sine.T], [sine.T, cosine.T]])
    forward_x = np.zeros((2, 2 * GRID, PENCILS, 16))
    inverse_x = np.zeros((2, PENCILS, 16, 2 * GRID))
    for h in range(2):
        for s in range(PENCILS):
            for c in range(2):
                rows = slice(4 * h + c * SLAB, 4 * h + (c + 1) * SLAB)
                xs = slice(c * GRID + s * SLAB, c * GRID + (s + 1) * SLAB)
                forward_x[h, :, s, rows] = full_f[:, xs]
                inverse_x[h, s, rows, :] = full_i[xs, :]
    lanes = np.zeros((8, 4 * LANES), np.float32)
    lanes[1] = 1000.0
    for tile in range(4):
        base = tile * LANES
        lanes[0, base : base + WIDTH[tile]] = tile
        lanes[1, base : base + WIDTH[tile]] = KZ[: WIDTH[tile]]
        band, first, count = FILL[tile]
        base += WIDTH[tile]
        lanes[0, base : base + count] = band
        lanes[1, base : base + count] = KZ[first : first + count]
    return dict(
        forward_z=halves(forward_z.reshape(2 * LANES, 2 * LANES)),
        inverse_z=halves(inverse_z.reshape(2 * LANES, 2 * LANES)),
        forward_y=halves(forward_y),
        inverse_y=halves(inverse_y),
        forward_x=halves(forward_x.reshape(2, 2 * GRID, 256)),
        inverse_x=halves(inverse_x.reshape(2, 256, 2 * GRID)),
        lanes=lanes,
    )


TABLES = build_tables()


def place():
    kpair = lax.axis_index("kpair")
    band = lax.axis_index("band")
    pencil = lax.axis_index("pencil")
    return kpair, band, pencil


def partners(kpair, band):
    core = kpair % 2
    chip = (kpair // 2) * 2 + band
    right_core = jnp.where(chip == 0, 1 - core, core)
    left_core = jnp.where(chip == 1, core, 1 - core)
    right = ((chip + 1) % 4 // 2) * 2 + right_core
    left = ((chip + 3) % 4 // 2) * 2 + left_core
    return right, left


def product3(left_high, left_low, right_high, right_low):
    dot = lambda a, b: jnp.dot(a, b, preferred_element_type=f32)
    return dot(left_high, right_high) + (dot(left_high, right_low) + dot(left_low, right_high))


def lane_index(rows):
    return lax.broadcasted_iota(jnp.int32, (rows, LANES), 1)


def chunk_row(tile, part, x):
    return (tile % 2) * CHUNK + (tile // 2) * 12 + part * SLAB + x


VMEM_LIMIT = 12 * 1024 * 1024


SPACE = {"vmem": pltpu.VMEM, "hbm": pltpu.HBM}


def kept_in(place, array):
    return pltpu.with_memory_space_constraint(array, SPACE[place]) if place in SPACE else array


class Fetched:
    def __init__(self, source, target, semaphore):
        self.target = target
        self.copy = pltpu.make_async_copy(source, target, semaphore)
        self.copy.start()
        self.pending = True

    def get(self):
        if self.pending:
            self.copy.wait()
            self.pending = False
        return self.target


class Ready:
    def __init__(self, ref):
        self.ref = ref

    def get(self):
        return self.ref


def call(kernel, out_shapes, scratch, args, interpret=False):
    places = [place for place, _ in args]
    arrays = [jnp.asarray(array) for _, array in args]
    specs = {
        "smem": pl.BlockSpec(memory_space=pltpu.SMEM),
        "vmem": pl.BlockSpec(memory_space=pltpu.VMEM),
        "hbm": pl.BlockSpec(memory_space=pltpu.HBM),
    }
    remote = [array for place, array in zip(places, arrays) if place == "hbm"]
    n_in, n_out = len(args), len(out_shapes)

    def entry(*refs):
        inputs, outputs = refs[:n_in], refs[n_in : n_in + n_out]
        rest = refs[n_in + n_out :]
        targets, semaphores, own_scratch = rest[: len(remote)], rest[len(remote)], rest[len(remote) + 1 :]
        handles, k = [], 0
        for place, ref in zip(places, inputs):
            if place == "hbm":
                handles.append(Fetched(ref, targets[k], semaphores.at[k]))
                k += 1
            else:
                handles.append(Ready(ref))
        kernel(*handles, *outputs, *own_scratch)

    return pl.pallas_call(
        entry,
        out_shape=out_shapes,
        in_specs=[specs[place] for place in places],
        out_specs=[specs["vmem"]] * n_out,
        scratch_shapes=[pltpu.VMEM(array.shape, array.dtype) for array in remote]
        + [pltpu.SemaphoreType.DMA((max(1, len(remote)),))]
        + scratch,
        interpret=interpret,
        compiler_params=pltpu.CompilerParams(vmem_limit_bytes=VMEM_LIMIT),
    )(*(kept_in(place, array) for place, array in zip(places, arrays)))


LOCAL = (("local", 0, 1),)
REMOTE = (("across", 1, 2), ("right", 0, 1), ("left", 0, 2))


def density_kernel(tasks, members, where, *refs):
    n = len(tasks)
    orbitals = refs[:members]
    z_table, y_table, out_ref, dens_ref, high_ref, low_ref = refs[members:]
    kpair, _, _ = where()
    lane = lane_index(24)
    lane16 = lane_index(16)
    for task, (kind, a, b) in enumerate(tasks):
        own_ref, far_ref = orbitals[a].get(), orbitals[b].get()
        own_real, own_imag = own_ref[0:ROWS, :], own_ref[ROWS : 2 * ROWS, :]
        far_real, far_imag = far_ref[0:ROWS, :], far_ref[ROWS : 2 * ROWS, :]
        real = far_real * own_real + far_imag * own_imag
        imag = far_real * own_imag - far_imag * own_real
        if kind == "local":
            packed = kpair % 2 == 1
            real = jnp.where(packed, own_real * own_real + own_imag * own_imag, real)
            imag = jnp.where(packed, far_real * far_real + far_imag * far_imag, imag)
        dens_ref[0:ROWS, :] = real
        dens_ref[ROWS : 2 * ROWS, :] = imag
        for c in range(2):
            cols = slice(c * LANES, (c + 1) * LANES)
            for x in range(SLAB):
                first = c * ROWS + x * 72
                t0, t1, t2 = (dens_ref[pl.ds(first + s, 24, stride=3), :] for s in range(3))
                rows = (
                    t0,
                    jnp.where(lane < 32, pltpu.roll(t0, 32, 1), pltpu.roll(t1, 32, 1)),
                    jnp.where(lane < 64, pltpu.roll(t1, 64, 1), pltpu.roll(t2, 64, 1)),
                    pltpu.roll(t2, 96, 1),
                )
                high, low = split(jnp.concatenate(rows, axis=0))
                high_ref[x * GRID : (x + 1) * GRID, cols] = high
                low_ref[x * GRID : (x + 1) * GRID, cols] = low
        z_ref = z_table.get()
        along_z = product3(high_ref[...], low_ref[...], z_ref[0], z_ref[1])
        high, low = split(along_z)
        high_ref[...] = high
        low_ref[...] = low
        y_ref = y_table.get()
        for x in range(0, SLAB, 2):
            def columns(ref):
                return jnp.concatenate(
                    [
                        jnp.concatenate(
                            [ref[v * GRID : (v + 1) * GRID, 0:LANES], ref[v * GRID : (v + 1) * GRID, LANES:]],
                            axis=0,
                        )
                        for v in (x, x + 1)
                    ],
                    axis=1,
                )

            along_y = product3(y_ref[0], y_ref[1], columns(high_ref), columns(low_ref))
            for v in range(2):
                for c in range(2):
                    bands = [
                        along_y[c * GRID + 16 * j : c * GRID + 16 * j + 16, v * LANES : (v + 1) * LANES]
                        for j in range(6)
                    ]
                    for tile in range(4):
                        band, start, _ = FILL[tile]
                        shift = (WIDTH[tile] - start) % LANES
                        value = jnp.where(lane16 < WIDTH[tile], bands[tile], pltpu.roll(bands[band], shift, 1))
                        row = task * 2 * CHUNK + chunk_row(tile, c, x + v)
                        out_ref[pl.ds(row, 16, stride=n * 2 * CHUNK), :] = value


def scratch_fields():
    return [
        pltpu.VMEM((2 * ROWS, LANES), f32),
        pltpu.VMEM((SLAB * GRID, 2 * LANES), bf16),
        pltpu.VMEM((SLAB * GRID, 2 * LANES), bf16),
    ]


def densities(tasks, orbitals, kept, where=place, interpret=False):
    n = len(tasks)
    (out,) = call(
        lambda *refs: density_kernel(tasks, len(orbitals), where, *refs),
        [kept((PENCILS * n * 2 * CHUNK, LANES), f32)],
        scratch_fields(),
        [*orbitals, ("hbm", TABLES["forward_z"]), ("hbm", TABLES["forward_y"])],
        interpret,
    )
    return out.reshape(PENCILS, n, 2, CHUNK, LANES)


def filter_kernel(groups, where, coords, *refs):
    chunks, (lanes, forward_table, inverse_table, out_ref) = refs[: len(groups)], refs[len(groups) :]
    coords_ref, lanes_ref = coords.get(), lanes.get()
    work = [(kind, chunks[g], i) for g, tasks in enumerate(groups) for i, (kind, _, _) in enumerate(tasks)]
    kpair, band, pencil = where()
    right, left = partners(kpair, band)
    points = {
        "local": (kpair, jnp.where(kpair % 2 == 1, kpair, kpair + 1)),
        "right": (kpair, right),
        "left": (kpair, left),
        "across": (right, left),
    }
    factor = (2.0 * math.pi / GRID) ** 2
    scale = -1.0 / (KPTS * NB) / GRID**3
    slot = lanes_ref[0:1, :]
    sign = (1 - 2 * (pencil % 2)).astype(f32)
    ky = sign * (8.0 * slot + (pencil // 2).astype(f32))
    ky = jnp.where(slot == jnp.where(pencil == 1, 0.0, -1.0), -48.0, ky)
    kz = lanes_ref[1:2, :]
    index = lax.broadcasted_iota(jnp.int32, (GRID, 2 * LANES), 0)
    kx = jnp.where(index < GRID // 2, index, index - GRID).astype(f32)
    for task, (kind, source, place) in enumerate(work):
        in_ref = source.get()
        here, there = points[kind]
        shift = [(coords_ref[here, a] - coords_ref[there, a]).astype(f32) * 0.25 for a in range(3)]
        plane = (ky + shift[1]) ** 2 + (kz + shift[2]) ** 2
        along_x = (kx + shift[0]) ** 2
        previous = None
        for h in range(2):
            rows = [
                in_ref[:, place, l, 8 * h : 8 * h + 16, :].reshape(256, LANES) for l in range(2)
            ]
            high, low = split(jnp.concatenate(rows, axis=1))
            forward_ref = forward_table.get()
            spectrum = product3(forward_ref[0, h], forward_ref[1, h], high, low)
            squared = along_x + plane[:, h * 256 : (h + 1) * 256]
            coulomb = jnp.where(
                squared <= RADIUS * RADIUS, 4.0 * math.pi / (factor * squared + SCREENING), 0.0
            ) * scale
            spectrum = jnp.concatenate([spectrum[:GRID] * coulomb, spectrum[GRID:] * coulomb], axis=0)
            high, low = split(spectrum)
            inverse_ref = inverse_table.get()
            back = product3(inverse_ref[0, h], inverse_ref[1, h], high, low).reshape(PENCILS, 16, 2 * LANES)
            for l in range(2):
                part = back[:, :, l * LANES : (l + 1) * LANES]
                if h == 0:
                    out_ref[:, task, l, 0:8, :] = part[:, 0:8]
                else:
                    out_ref[:, task, l, 16:24, :] = part[:, 8:16]
                    out_ref[:, task, l, 8:16, :] = part[:, 0:8] + previous[:, 8:16, l * LANES : (l + 1) * LANES]
            previous = back


def filtered(groups, coords, chunks, where=place, interpret=False):
    n = sum(len(tasks) for tasks in groups)
    (out,) = call(
        lambda *refs: filter_kernel(groups, where, *refs),
        [jax.ShapeDtypeStruct((PENCILS, n, 2, CHUNK, LANES), f32)],
        [],
        [
            ("smem", coords),
            *chunks,
            ("hbm", TABLES["lanes"]),
            ("hbm", TABLES["forward_x"]),
            ("hbm", TABLES["inverse_x"]),
        ],
        interpret,
    )
    return out


def potential_kernel(tasks, first, n, members, bases, where, chunks, *refs):
    in_ref = chunks.get()
    orbitals, refs = refs[:members], refs[members:]
    y_table, z_table, refs = refs[0], refs[1], refs[2:]
    started, refs = refs[:bases], refs[bases:]
    sum_refs = refs[:members]
    pot_ref, high_ref, low_ref = refs[members:]
    earlier = dict(enumerate(started))
    kpair, _, _ = where()
    lane = lane_index(24)
    lane16 = lane_index(16)
    for task, (kind, a, b) in enumerate(tasks, first):
        for x in range(0, SLAB, 2):
            pair = []
            for v in (x, x + 1):
                parts = []
                for c in range(2):
                    tiles = [
                        in_ref[pl.ds(task * 2 * CHUNK + chunk_row(t, c, v), 16, stride=n * 2 * CHUNK), :]
                        for t in range(4)
                    ]
                    bands = [jnp.where(lane16 < WIDTH[t], tiles[t], 0.0) for t in range(4)]
                    for (ta, tb) in ((3, 0), (1, 2)):
                        _, sa, ca = FILL[ta]
                        _, sb, cb = FILL[tb]
                        head = pltpu.roll(tiles[ta], (sa - WIDTH[ta]) % LANES, 1)
                        tail = pltpu.roll(tiles[tb], (sb - WIDTH[tb]) % LANES, 1)
                        bands.append(jnp.where(lane16 < ca, head, jnp.where(lane16 < ca + cb, tail, 0.0)))
                    parts += bands
                pair.append(jnp.concatenate(parts, axis=0))
            high, low = split(jnp.concatenate(pair, axis=1))
            y_ref = y_table.get()
            along_y = product3(y_ref[0], y_ref[1], high, low)
            high, low = split(along_y)
            for v in range(2):
                for c in range(2):
                    rows = slice((x + v) * GRID, (x + v + 1) * GRID)
                    cols = slice(c * LANES, (c + 1) * LANES)
                    high_ref[rows, cols] = high[c * GRID : (c + 1) * GRID, v * LANES : (v + 1) * LANES]
                    low_ref[rows, cols] = low[c * GRID : (c + 1) * GRID, v * LANES : (v + 1) * LANES]
        z_ref = z_table.get()
        along_z = product3(high_ref[...], low_ref[...], z_ref[0], z_ref[1])
        for c in range(2):
            for x in range(SLAB):
                v0, v1, v2, v3 = (
                    along_z[x * GRID + 24 * j : x * GRID + 24 * j + 24, c * LANES : (c + 1) * LANES]
                    for j in range(4)
                )
                v1, v2, v3 = pltpu.roll(v1, 96, 1), pltpu.roll(v2, 64, 1), pltpu.roll(v3, 32, 1)
                rows = (jnp.where(lane < 96, v0, v1), jnp.where(lane < 64, v1, v2), jnp.where(lane < 32, v2, v3))
                for s in range(3):
                    pot_ref[pl.ds(c * ROWS + x * 72 + s, 24, stride=3), :] = rows[s]
        own_ref, far_ref = orbitals[a].get(), orbitals[b].get()
        own_real, own_imag = own_ref[0:ROWS, :], own_ref[ROWS : 2 * ROWS, :]
        far_real, far_imag = far_ref[0:ROWS, :], far_ref[ROWS : 2 * ROWS, :]
        pot_real, pot_imag = pot_ref[0:ROWS, :], pot_ref[ROWS : 2 * ROWS, :]
        here_real = far_real * pot_real - far_imag * pot_imag
        here_imag = far_real * pot_imag + far_imag * pot_real
        there_real = own_real * pot_real + own_imag * pot_imag
        there_imag = own_imag * pot_real - own_real * pot_imag
        if kind == "local":
            packed = kpair % 2 == 1
            here_real = jnp.where(packed, own_real * pot_real, here_real)
            here_imag = jnp.where(packed, own_imag * pot_real, here_imag)
            there_real = jnp.where(packed, far_real * pot_imag, there_real)
            there_imag = jnp.where(packed, far_imag * pot_imag, there_imag)
        for member, real, imag in ((a, here_real, here_imag), (b, there_real, there_imag)):
            if member in earlier:
                base_ref = earlier[member].get()
                real = real + base_ref[0:ROWS, :]
                imag = imag + base_ref[ROWS : 2 * ROWS, :]
            earlier[member] = Ready(sum_refs[member])
            sum_refs[member][0:ROWS, :] = real
            sum_refs[member][ROWS : 2 * ROWS, :] = imag


def potentials(tasks, first, chunks, orbitals, kept, bases=(), where=place, interpret=False):
    n = chunks.shape[1]
    return call(
        lambda *refs: potential_kernel(tasks, first, n, len(orbitals), len(bases), where, *refs),
        kept,
        scratch_fields(),
        [
            ("vmem", chunks.reshape(PENCILS * n * 2 * CHUNK, LANES)),
            *orbitals,
            ("hbm", TABLES["inverse_y"]),
            ("hbm", TABLES["inverse_z"]),
            *bases,
        ],
        interpret,
    )


def line(chip, core):
    chip %= 4
    return (chip // 2) * 4 + core * 2 + chip % 2


TURN = (1, 0, 0, 0)


def route(kind):
    pairs = []
    for chip in range(4):
        for core in range(2):
            if kind == "local":
                source = line(chip, 1 - core)
            elif kind == "right":
                source = line(chip + 1, core ^ TURN[chip])
            else:
                source = line(chip - 1, core ^ (1 - TURN[chip - 1]))
            pairs.append((source, line(chip, core)))
    return pairs


def fetch(kind, block):
    return lax.ppermute(block, ("kpair", "band"), route(kind))


def give_back(kind, block):
    return lax.ppermute(block, ("kpair", "band"), [(b, a) for a, b in route(kind)])


def transpose(chunks):
    return lax.all_to_all(chunks, "pencil", 0, 0, tiled=True)


DENSE = (2 * ROWS, LANES)


def body(orbitals, kcoords):
    own = orbitals.reshape(DENSE)
    right, left, other = fetch("right", own), fetch("left", own), fetch("local", own)
    near = [("hbm", own), ("vmem", other)]
    far = [("hbm", own), ("vmem", right), ("vmem", left)]
    chunks_near = densities(LOCAL, near, pltpu.HBM)
    sent_near = transpose(chunks_near)
    chunks_far = densities(REMOTE, far, jax.ShapeDtypeStruct)
    sent_far = transpose(chunks_far)
    spectrum = filtered((REMOTE, LOCAL), kcoords, [("vmem", sent_far), ("vmem", sent_near)])
    back = transpose(spectrum)
    kept = [jax.ShapeDtypeStruct(DENSE, f32)] * 3
    far_sum, for_right, for_left = potentials(REMOTE, 0, back, far, kept)
    from_right = give_back("right", for_right)
    from_left = give_back("left", for_left)
    kept = [jax.ShapeDtypeStruct(DENSE, f32)] * 2
    own_sum, for_other = potentials(LOCAL, len(REMOTE), back, near, kept, [("vmem", far_sum)])
    from_other = give_back("local", for_other)
    out = own_sum + from_other + (from_right + from_left)
    return out.reshape(2, 1, 1, SLAB, GRID * GRID)


def solution(mesh):
    in_specs = (P(None, "kpair", "band", "pencil", None), P())
    out_specs = P(None, "kpair", "band", "pencil", None)
    return jax.shard_map(body, mesh=mesh, in_specs=in_specs, out_specs=out_specs, check_vma=False)
```

```python
import math

import jax
import jax.numpy as jnp
import numpy as np
from jax import lax
from jax.experimental import pallas as pl
from jax.experimental.pallas import tpu as pltpu
from jax.sharding import PartitionSpec as P

GRID = 96
NB = 2
KPTS = 4
SCREENING = 0.5
RADIUS = GRID // 2 - 1
PENCILS = 16
SLAB = GRID // PENCILS
LANES = 128
ROWS = SLAB * GRID * GRID // LANES
CHUNK = 24

f32 = jnp.float32
bf16 = jnp.bfloat16

KZ = np.array([0] + [s * i for i in range(1, 48) for s in (1, -1)])
KY = np.array([[(8 * j + d // 2) * (1 - 2 * (d % 2)) for d in range(16)] for j in range(6)])
KY[0, 1] = -48
WIDTH = [
    2 * min(RADIUS, int(0.75 + math.sqrt(RADIUS**2 - max(0.0, 8 * j - 0.75) ** 2))) + 1
    for j in range(6)
]
SPLIT4 = LANES - WIDTH[3]
SPLIT5 = LANES - WIDTH[1]
FILL = {
    3: (4, 0, SPLIT4),
    0: (4, SPLIT4, WIDTH[4] - SPLIT4),
    1: (5, 0, SPLIT5),
    2: (5, SPLIT5, WIDTH[5] - SPLIT5),
}
for tile, (band, first, count) in FILL.items():
    assert WIDTH[tile] + count <= LANES


def split(values):
    high = jnp.asarray(values, f32).astype(bf16)
    low = (jnp.asarray(values, f32) - high.astype(f32)).astype(bf16)
    return high, low


def halves(table):
    table = np.asarray(table, np.float32)
    high = table.astype(bf16)
    low = (table - high.astype(np.float32)).astype(bf16)
    return np.stack([high, low])


def angles(rows, cols):
    product = np.outer(rows, cols) % GRID
    angle = product * (2.0 * math.pi / GRID)
    return np.cos(angle), np.sin(angle)


def build_tables():
    cosine, sine = angles(np.arange(GRID), KZ)
    forward_z = np.zeros((2, LANES, 2, LANES))
    inverse_z = np.zeros((2, LANES, 2, LANES))
    n = len(KZ)
    forward_z[0, :GRID, 0, :n] = cosine
    forward_z[1, :GRID, 0, :n] = sine
    forward_z[0, :GRID, 1, :n] = -sine
    forward_z[1, :GRID, 1, :n] = cosine
    inverse_z[0, :n, 0, :GRID] = cosine.T
    inverse_z[1, :n, 0, :GRID] = -sine.T
    inverse_z[0, :n, 1, :GRID] = sine.T
    inverse_z[1, :n, 1, :GRID] = cosine.T
    order_y = np.array([4 * g + j for j in range(4) for g in range(24)])
    cosine, sine = angles(KY.reshape(-1), order_y)
    forward_y = np.block([[cosine, sine], [-sine, cosine]])
    inverse_y = np.block([[cosine.T, -sine.T], [sine.T, cosine.T]])
    freq = np.where(np.arange(GRID) < GRID // 2, np.arange(GRID), np.arange(GRID) - GRID)
    cosine, sine = angles(freq, np.arange(GRID))
    full_f = np.block([[cosine, sine], [-sine, cosine]])
    full_i = np.block([[cosine.T, -sine.T], [sine.T, cosine.T]])
    forward_x = np.zeros((2, 2 * GRID, PENCILS, 16))
    inverse_x = np.zeros((2, PENCILS, 16, 2 * GRID))
    for h in range(2):
        for s in range(PENCILS):
            for c in range(2):
                rows = slice(4 * h + c * SLAB, 4 * h + (c + 1) * SLAB)
                xs = slice(c * GRID + s * SLAB, c * GRID + (s + 1) * SLAB)
                forward_x[h, :, s, rows] = full_f[:, xs]
                inverse_x[h, s, rows, :] = full_i[xs, :]
    lanes = np.zeros((8, 4 * LANES), np.float32)
    lanes[1] = 1000.0
    for tile in range(4):
        base = tile * LANES
        lanes[0, base : base + WIDTH[tile]] = tile
        lanes[1, base : base + WIDTH[tile]] = KZ[: WIDTH[tile]]
        band, first, count = FILL[tile]
        base += WIDTH[tile]
        lanes[0, base : base + count] = band
        lanes[1, base : base + count] = KZ[first : first + count]
    return dict(
        forward_z=halves(forward_z.reshape(2 * LANES, 2 * LANES)),
        inverse_z=halves(inverse_z.reshape(2 * LANES, 2 * LANES)),
        forward_y=halves(forward_y),
        inverse_y=halves(inverse_y),
        forward_x=halves(forward_x.reshape(2, 2 * GRID, 256)).swapaxes(0, 1),
        inverse_x=halves(inverse_x.reshape(2, 256, 2 * GRID)).swapaxes(0, 1),
        lanes=lanes,
    )


TABLES = build_tables()


def place():
    kpair = lax.axis_index("kpair")
    band = lax.axis_index("band")
    pencil = lax.axis_index("pencil")
    return kpair, band, pencil


def partners(kpair, band):
    core = kpair % 2
    chip = (kpair // 2) * 2 + band
    right_core = jnp.where(chip == 0, 1 - core, core)
    left_core = jnp.where(chip == 1, core, 1 - core)
    right = ((chip + 1) % 4 // 2) * 2 + right_core
    left = ((chip + 3) % 4 // 2) * 2 + left_core
    return right, left


def data_product(left_high, left_low, table_ref):
    rows = left_high.shape[0]
    dot = lambda a, b: jnp.dot(a, b, preferred_element_type=f32)
    both = dot(jnp.concatenate([left_high, left_low], axis=0), table_ref[0])
    return both[:rows] + (both[rows:] + dot(left_high, table_ref[1]))


def table_product(table, right_high, right_low):
    rows = table.shape[0] // 2
    dot = lambda a, b: jnp.dot(a, b, preferred_element_type=f32)
    both = dot(table, right_high)
    return both[:rows] + (both[rows:] + dot(table[:rows], right_low))


def lane_index(rows):
    return lax.broadcasted_iota(jnp.int32, (rows, LANES), 1)


def chunk_row(tile, part, x):
    return (tile % 2) * CHUNK + (tile // 2) * 12 + part * SLAB + x


VMEM_LIMIT = 12 * 1024 * 1024


SPACE = {"vmem": pltpu.VMEM, "hbm": pltpu.HBM}


def kept_in(place, array):
    return pltpu.with_memory_space_constraint(array, SPACE[place]) if place in SPACE else array


class Fetched:
    def __init__(self, source, target, semaphore):
        self.target = target
        self.copy = pltpu.make_async_copy(source, target, semaphore)
        self.copy.start()
        self.pending = True

    def get(self):
        if self.pending:
            self.copy.wait()
            self.pending = False
        return self.target


class Ready:
    def __init__(self, ref):
        self.ref = ref

    def get(self):
        return self.ref


def call(kernel, out_shapes, scratch, args, interpret=False):
    places = [place for place, _ in args]
    arrays = [jnp.asarray(array) for _, array in args]
    specs = {
        "smem": pl.BlockSpec(memory_space=pltpu.SMEM),
        "vmem": pl.BlockSpec(memory_space=pltpu.VMEM),
        "hbm": pl.BlockSpec(memory_space=pltpu.HBM),
    }
    remote = [array for place, array in zip(places, arrays) if place == "hbm"]
    n_in, n_out = len(args), len(out_shapes)

    def entry(*refs):
        inputs, outputs = refs[:n_in], refs[n_in : n_in + n_out]
        rest = refs[n_in + n_out :]
        targets, semaphores, own_scratch = rest[: len(remote)], rest[len(remote)], rest[len(remote) + 1 :]
        handles, k = [], 0
        for place, ref in zip(places, inputs):
            if place == "hbm":
                handles.append(Fetched(ref, targets[k], semaphores.at[k]))
                k += 1
            else:
                handles.append(Ready(ref))
        for handle in handles:
            handle.get()
        kernel(*handles, *outputs, *own_scratch)

    return pl.pallas_call(
        entry,
        out_shape=out_shapes,
        in_specs=[specs[place] for place in places],
        out_specs=[specs["vmem"]] * n_out,
        scratch_shapes=[pltpu.VMEM(array.shape, array.dtype) for array in remote]
        + [pltpu.SemaphoreType.DMA((max(1, len(remote)),))]
        + scratch,
        interpret=interpret,
        compiler_params=pltpu.CompilerParams(vmem_limit_bytes=VMEM_LIMIT),
    )(*(kept_in(place, array) for place, array in zip(places, arrays)))


LOCAL = (("local", 0, 1),)
REMOTE = (("across", 1, 2), ("right", 0, 1), ("left", 0, 2))


def strided(part, x, s):
    return pl.ds(part * ROWS + x * 72 + s, 24, stride=3)


def density_kernel(tasks, members, where, *refs):
    n = len(tasks)
    orbitals = refs[:members]
    z_table, y_table, out_ref = refs[members:]
    kpair, _, _ = where()
    lane = lane_index(24)
    lane16 = lane_index(16)
    for task, (kind, a, b) in enumerate(tasks):
        own_ref, far_ref = orbitals[a].get(), orbitals[b].get()
        for x in range(0, SLAB, 2):
            planes = []
            for v in (x, x + 1):
                tiles = ([], [])
                for s in range(3):
                    own_real, own_imag = own_ref[strided(0, v, s), :], own_ref[strided(1, v, s), :]
                    far_real, far_imag = far_ref[strided(0, v, s), :], far_ref[strided(1, v, s), :]
                    real = far_real * own_real + far_imag * own_imag
                    imag = far_real * own_imag - far_imag * own_real
                    if kind == "local":
                        packed = kpair % 2 == 1
                        real = jnp.where(packed, own_real * own_real + own_imag * own_imag, real)
                        imag = jnp.where(packed, far_real * far_real + far_imag * far_imag, imag)
                    tiles[0].append(real)
                    tiles[1].append(imag)
                parts = []
                for t0, t1, t2 in tiles:
                    rows = (
                        t0,
                        jnp.where(lane < 32, pltpu.roll(t0, 32, 1), pltpu.roll(t1, 32, 1)),
                        jnp.where(lane < 64, pltpu.roll(t1, 64, 1), pltpu.roll(t2, 64, 1)),
                        pltpu.roll(t2, 96, 1),
                    )
                    parts.append(jnp.concatenate(rows, axis=0))
                planes.append(jnp.concatenate(parts, axis=1))
            along_z = data_product(*split(jnp.concatenate(planes, axis=0)), z_table.get())
            columns = jnp.concatenate(
                [
                    jnp.concatenate(
                        [along_z[v * GRID : (v + 1) * GRID, c * LANES : (c + 1) * LANES] for c in range(2)], axis=0
                    )
                    for v in range(2)
                ],
                axis=1,
            )
            along_y = table_product(y_table.get()[...].reshape(4 * GRID, 2 * GRID), *split(columns))
            for v in range(2):
                for c in range(2):
                    bands = [
                        along_y[c * GRID + 16 * j : c * GRID + 16 * j + 16, v * LANES : (v + 1) * LANES]
                        for j in range(6)
                    ]
                    for tile in range(4):
                        band, start, _ = FILL[tile]
                        shift = (WIDTH[tile] - start) % LANES
                        value = jnp.where(lane16 < WIDTH[tile], bands[tile], pltpu.roll(bands[band], shift, 1))
                        row = task * 2 * CHUNK + chunk_row(tile, c, x + v)
                        out_ref[pl.ds(row, 16, stride=n * 2 * CHUNK), :] = value


def densities(tasks, orbitals, kept, early, where=place, interpret=False):
    n = len(tasks)
    (out,) = call(
        lambda *refs: density_kernel(tasks, len(orbitals), where, *refs),
        [kept((PENCILS * n * 2 * CHUNK, LANES), f32)],
        [],
        [*orbitals, (early, TABLES["forward_z"]), (early, TABLES["forward_y"])],
        interpret,
    )
    return out.reshape(PENCILS, n, 2, CHUNK, LANES)


def filter_kernel(groups, where, coords, *refs):
    chunks, (lanes, forward_table, inverse_table, out_ref) = refs[: len(groups)], refs[len(groups) :]
    coords_ref, lanes_ref = coords.get(), lanes.get()
    work = [(kind, chunks[g], i) for g, tasks in enumerate(groups) for i, (kind, _, _) in enumerate(tasks)]
    kpair, band, pencil = where()
    right, left = partners(kpair, band)
    points = {
        "local": (kpair, jnp.where(kpair % 2 == 1, kpair, kpair + 1)),
        "right": (kpair, right),
        "left": (kpair, left),
        "across": (right, left),
    }
    factor = (2.0 * math.pi / GRID) ** 2
    scale = -1.0 / (KPTS * NB) / GRID**3
    slot = lanes_ref[0:1, :]
    sign = (1 - 2 * (pencil % 2)).astype(f32)
    ky = sign * (8.0 * slot + (pencil // 2).astype(f32))
    ky = jnp.where(slot == jnp.where(pencil == 1, 0.0, -1.0), -48.0, ky)
    kz = lanes_ref[1:2, :]
    index = lax.broadcasted_iota(jnp.int32, (GRID, 2 * LANES), 0)
    kx = jnp.where(index < GRID // 2, index, index - GRID).astype(f32)
    for task, (kind, source, place) in enumerate(work):
        in_ref = source.get()
        here, there = points[kind]
        shift = [(coords_ref[here, a] - coords_ref[there, a]).astype(f32) * 0.25 for a in range(3)]
        plane = (ky + shift[1]) ** 2 + (kz + shift[2]) ** 2
        along_x = (kx + shift[0]) ** 2
        previous = None
        for h in range(2):
            rows = [
                in_ref[:, place, l, 8 * h : 8 * h + 16, :].reshape(256, LANES) for l in range(2)
            ]
            high, low = split(jnp.concatenate(rows, axis=1))
            forward_ref = forward_table.get()
            spectrum = table_product(forward_ref[h].reshape(4 * GRID, 256), high, low)
            squared = along_x + plane[:, h * 256 : (h + 1) * 256]
            coulomb = jnp.where(
                squared <= RADIUS * RADIUS, 4.0 * math.pi / (factor * squared + SCREENING), 0.0
            ) * scale
            spectrum = jnp.concatenate([spectrum[:GRID] * coulomb, spectrum[GRID:] * coulomb], axis=0)
            high, low = split(spectrum)
            inverse_ref = inverse_table.get()
            back = table_product(inverse_ref[h].reshape(512, 2 * GRID), high, low).reshape(PENCILS, 16, 2 * LANES)
            for l in range(2):
                part = back[:, :, l * LANES : (l + 1) * LANES]
                if h == 0:
                    out_ref[:, task, l, 0:8, :] = part[:, 0:8]
                else:
                    out_ref[:, task, l, 16:24, :] = part[:, 8:16]
                    out_ref[:, task, l, 8:16, :] = part[:, 0:8] + previous[:, 8:16, l * LANES : (l + 1) * LANES]
            previous = back


def filtered(groups, coords, chunks, where=place, interpret=False):
    n = sum(len(tasks) for tasks in groups)
    (out,) = call(
        lambda *refs: filter_kernel(groups, where, *refs),
        [jax.ShapeDtypeStruct((PENCILS, n, 2, CHUNK, LANES), f32)],
        [],
        [
            ("smem", coords),
            *chunks,
            ("vmem", TABLES["lanes"]),
            ("vmem", TABLES["forward_x"]),
            ("vmem", TABLES["inverse_x"]),
        ],
        interpret,
    )
    return out


def potential_kernel(tasks, first, n, members, bases, where, chunks, *refs):
    in_ref = chunks.get()
    orbitals, refs = refs[:members], refs[members:]
    y_table, z_table, refs = refs[0], refs[1], refs[2:]
    started, sum_refs = refs[:bases], refs[bases:]
    earlier = dict(enumerate(started))
    kpair, _, _ = where()
    lane = lane_index(24)
    lane16 = lane_index(16)
    for task, (kind, a, b) in enumerate(tasks, first):
        for x in range(0, SLAB, 2):
            pair = []
            for v in (x, x + 1):
                parts = []
                for c in range(2):
                    tiles = [
                        in_ref[pl.ds(task * 2 * CHUNK + chunk_row(t, c, v), 16, stride=n * 2 * CHUNK), :]
                        for t in range(4)
                    ]
                    bands = [jnp.where(lane16 < WIDTH[t], tiles[t], 0.0) for t in range(4)]
                    for (ta, tb) in ((3, 0), (1, 2)):
                        _, sa, ca = FILL[ta]
                        _, sb, cb = FILL[tb]
                        head = pltpu.roll(tiles[ta], (sa - WIDTH[ta]) % LANES, 1)
                        tail = pltpu.roll(tiles[tb], (sb - WIDTH[tb]) % LANES, 1)
                        bands.append(jnp.where(lane16 < ca, head, jnp.where(lane16 < ca + cb, tail, 0.0)))
                    parts += bands
                pair.append(jnp.concatenate(parts, axis=0))
            columns = jnp.concatenate(pair, axis=1)
            along_y = table_product(y_table.get()[...].reshape(4 * GRID, 2 * GRID), *split(columns))
            planes = jnp.concatenate(
                [
                    jnp.concatenate(
                        [along_y[c * GRID : (c + 1) * GRID, v * LANES : (v + 1) * LANES] for c in range(2)], axis=1
                    )
                    for v in range(2)
                ],
                axis=0,
            )
            along_z = data_product(*split(planes), z_table.get())
            own_ref, far_ref = orbitals[a].get(), orbitals[b].get()
            for v in range(2):
                tiles = []
                for c in range(2):
                    v0, v1, v2, v3 = (
                        along_z[v * GRID + 24 * j : v * GRID + 24 * j + 24, c * LANES : (c + 1) * LANES]
                        for j in range(4)
                    )
                    v1, v2, v3 = pltpu.roll(v1, 96, 1), pltpu.roll(v2, 64, 1), pltpu.roll(v3, 32, 1)
                    tiles.append(
                        (jnp.where(lane < 96, v0, v1), jnp.where(lane < 64, v1, v2), jnp.where(lane < 32, v2, v3))
                    )
                for s in range(3):
                    at_real, at_imag = strided(0, x + v, s), strided(1, x + v, s)
                    own_real, own_imag = own_ref[at_real, :], own_ref[at_imag, :]
                    far_real, far_imag = far_ref[at_real, :], far_ref[at_imag, :]
                    pot_real, pot_imag = tiles[0][s], tiles[1][s]
                    here_real = far_real * pot_real - far_imag * pot_imag
                    here_imag = far_real * pot_imag + far_imag * pot_real
                    there_real = own_real * pot_real + own_imag * pot_imag
                    there_imag = own_imag * pot_real - own_real * pot_imag
                    if kind == "local":
                        packed = kpair % 2 == 1
                        here_real = jnp.where(packed, own_real * pot_real, here_real)
                        here_imag = jnp.where(packed, own_imag * pot_real, here_imag)
                        there_real = jnp.where(packed, far_real * pot_imag, there_real)
                        there_imag = jnp.where(packed, far_imag * pot_imag, there_imag)
                    for member, real, imag in ((a, here_real, here_imag), (b, there_real, there_imag)):
                        if member in earlier:
                            base_ref = earlier[member].get()
                            real = real + base_ref[at_real, :]
                            imag = imag + base_ref[at_imag, :]
                        sum_refs[member][at_real, :] = real
                        sum_refs[member][at_imag, :] = imag
        for member in (a, b):
            earlier[member] = Ready(sum_refs[member])


def potentials(tasks, first, chunks, orbitals, kept, early, bases=(), where=place, interpret=False):
    n = chunks.shape[1]
    return call(
        lambda *refs: potential_kernel(tasks, first, n, len(orbitals), len(bases), where, *refs),
        kept,
        [],
        [
            ("vmem", chunks.reshape(PENCILS * n * 2 * CHUNK, LANES)),
            *orbitals,
            (early, TABLES["inverse_y"]),
            (early, TABLES["inverse_z"]),
            *bases,
        ],
        interpret,
    )


def line(chip, core):
    chip %= 4
    return (chip // 2) * 4 + core * 2 + chip % 2


TURN = (1, 0, 0, 0)


def route(kind):
    pairs = []
    for chip in range(4):
        for core in range(2):
            if kind == "local":
                source = line(chip, 1 - core)
            elif kind == "right":
                source = line(chip + 1, core ^ TURN[chip])
            else:
                source = line(chip - 1, core ^ (1 - TURN[chip - 1]))
            pairs.append((source, line(chip, core)))
    return pairs


def fetch(kind, block):
    return lax.ppermute(block, ("kpair", "band"), route(kind))


def give_back(kind, block):
    return lax.ppermute(block, ("kpair", "band"), [(b, a) for a, b in route(kind)])


def transpose(chunks):
    return lax.all_to_all(chunks, "pencil", 0, 0, tiled=True)


DENSE = (2 * ROWS, LANES)


def body(orbitals, kcoords):
    own = orbitals.reshape(DENSE)
    right, left, other = fetch("right", own), fetch("left", own), fetch("local", own)
    near = [("hbm", own), ("vmem", other)]
    far = [("vmem", own), ("vmem", right), ("vmem", left)]
    chunks_near = densities(LOCAL, near, pltpu.HBM, "hbm")
    sent_near = transpose(chunks_near)
    chunks_far = densities(REMOTE, far, jax.ShapeDtypeStruct, "vmem")
    sent_far = transpose(chunks_far)
    spectrum = filtered((REMOTE, LOCAL), kcoords, [("vmem", sent_far), ("vmem", sent_near)])
    back = transpose(spectrum)
    kept = [jax.ShapeDtypeStruct(DENSE, f32)] * 3
    far_sum, for_right, for_left = potentials(REMOTE, 0, back, far, kept, "vmem")
    from_right = give_back("right", for_right)
    from_left = give_back("left", for_left)
    kept = [jax.ShapeDtypeStruct(DENSE, f32)] * 2
    own_sum, for_other = potentials(LOCAL, len(REMOTE), back, near, kept, "hbm", [("vmem", far_sum)])
    from_other = give_back("local", for_other)
    out = own_sum + from_other + (from_right + from_left)
    return out.reshape(2, 1, 1, SLAB, GRID * GRID)


def solution(mesh):
    in_specs = (P(None, "kpair", "band", "pencil", None), P())
    out_specs = P(None, "kpair", "band", "pencil", None)
    return jax.shard_map(body, mesh=mesh, in_specs=in_specs, out_specs=out_specs, check_vma=False)
```

```python
import math

import jax
import jax.numpy as jnp
import numpy as np
from jax import lax
from jax.experimental import pallas as pl
from jax.experimental.pallas import tpu as pltpu
from jax.sharding import PartitionSpec as P

GRID = 96
NB = 2
KPTS = 4
SCREENING = 0.5
RADIUS = GRID // 2 - 1
PENCILS = 16
SLAB = GRID // PENCILS
LANES = 128
ROWS = SLAB * GRID * GRID // LANES
CHUNK = 24

f32 = jnp.float32
bf16 = jnp.bfloat16

KZ = np.array([0] + [s * i for i in range(1, 48) for s in (1, -1)])
KY = np.array([[(8 * j + d // 2) * (1 - 2 * (d % 2)) for d in range(16)] for j in range(6)])
KY[0, 1] = -48
WIDTH = [
    2 * min(RADIUS, int(0.75 + math.sqrt(RADIUS**2 - max(0.0, 8 * j - 0.75) ** 2))) + 1
    for j in range(6)
]
SPLIT4 = LANES - WIDTH[3]
SPLIT5 = LANES - WIDTH[1]
FILL = {
    3: (4, 0, SPLIT4),
    0: (4, SPLIT4, WIDTH[4] - SPLIT4),
    1: (5, 0, SPLIT5),
    2: (5, SPLIT5, WIDTH[5] - SPLIT5),
}
for tile, (band, first, count) in FILL.items():
    assert WIDTH[tile] + count <= LANES


def split(values):
    high = jnp.asarray(values, f32).astype(bf16)
    low = (jnp.asarray(values, f32) - high.astype(f32)).astype(bf16)
    return high, low


def halves(table):
    table = np.asarray(table, np.float32)
    high = table.astype(bf16)
    low = (table - high.astype(np.float32)).astype(bf16)
    return np.stack([high, low])


def angles(rows, cols):
    product = np.outer(rows, cols) % GRID
    angle = product * (2.0 * math.pi / GRID)
    return np.cos(angle), np.sin(angle)


def build_tables():
    cosine, sine = angles(np.arange(GRID), KZ)
    forward_z = np.zeros((2, LANES, 2, LANES))
    inverse_z = np.zeros((2, LANES, 2, LANES))
    n = len(KZ)
    forward_z[0, :GRID, 0, :n] = cosine
    forward_z[1, :GRID, 0, :n] = sine
    forward_z[0, :GRID, 1, :n] = -sine
    forward_z[1, :GRID, 1, :n] = cosine
    inverse_z[0, :n, 0, :GRID] = cosine.T
    inverse_z[1, :n, 0, :GRID] = -sine.T
    inverse_z[0, :n, 1, :GRID] = sine.T
    inverse_z[1, :n, 1, :GRID] = cosine.T
    order_y = np.array([4 * g + j for j in range(4) for g in range(24)])
    cosine, sine = angles(KY.reshape(-1), order_y)
    forward_y = np.block([[cosine, sine], [-sine, cosine]])
    inverse_y = np.block([[cosine.T, -sine.T], [sine.T, cosine.T]])
    freq = np.where(np.arange(GRID) < GRID // 2, np.arange(GRID), np.arange(GRID) - GRID)
    cosine, sine = angles(freq, np.arange(GRID))
    full_f = np.block([[cosine, sine], [-sine, cosine]])
    full_i = np.block([[cosine.T, -sine.T], [sine.T, cosine.T]])
    forward_x = np.zeros((2, 2 * GRID, PENCILS, 16))
    inverse_x = np.zeros((2, PENCILS, 16, 2 * GRID))
    for h in range(2):
        for s in range(PENCILS):
            for c in range(2):
                rows = slice(4 * h + c * SLAB, 4 * h + (c + 1) * SLAB)
                xs = slice(c * GRID + s * SLAB, c * GRID + (s + 1) * SLAB)
                forward_x[h, :, s, rows] = full_f[:, xs]
                inverse_x[h, s, rows, :] = full_i[xs, :]
    lanes = np.zeros((8, 4 * LANES), np.float32)
    lanes[1] = 1000.0
    for tile in range(4):
        base = tile * LANES
        lanes[0, base : base + WIDTH[tile]] = tile
        lanes[1, base : base + WIDTH[tile]] = KZ[: WIDTH[tile]]
        band, first, count = FILL[tile]
        base += WIDTH[tile]
        lanes[0, base : base + count] = band
        lanes[1, base : base + count] = KZ[first : first + count]
    return dict(
        forward_z=halves(forward_z.reshape(2 * LANES, 2 * LANES)),
        inverse_z=halves(inverse_z.reshape(2 * LANES, 2 * LANES)),
        forward_y=halves(forward_y),
        inverse_y=halves(inverse_y),
        forward_x=halves(forward_x.reshape(2, 2 * GRID, 256)).swapaxes(0, 1),
        inverse_x=halves(inverse_x.reshape(2, 256, 2 * GRID)).swapaxes(0, 1),
        lanes=lanes,
    )


TABLES = build_tables()


def place():
    kpair = lax.axis_index("kpair")
    band = lax.axis_index("band")
    pencil = lax.axis_index("pencil")
    return kpair, band, pencil


def partners(kpair, band):
    core = kpair % 2
    chip = (kpair // 2) * 2 + band
    right_core = jnp.where(chip == 0, 1 - core, core)
    left_core = jnp.where(chip == 1, core, 1 - core)
    right = ((chip + 1) % 4 // 2) * 2 + right_core
    left = ((chip + 3) % 4 // 2) * 2 + left_core
    return right, left


def data_product(left_high, left_low, table_ref):
    rows = left_high.shape[0]
    dot = lambda a, b: jnp.dot(a, b, preferred_element_type=f32)
    both = dot(jnp.concatenate([left_high, left_low], axis=0), table_ref[0])
    return both[:rows] + (both[rows:] + dot(left_high, table_ref[1]))


def table_product(table, right_high, right_low):
    rows = table.shape[0] // 2
    dot = lambda a, b: jnp.dot(a, b, preferred_element_type=f32)
    both = dot(table, right_high)
    return both[:rows] + (both[rows:] + dot(table[:rows], right_low))


def lane_index(rows):
    return lax.broadcasted_iota(jnp.int32, (rows, LANES), 1)


def chunk_row(tile, part, x):
    return (tile % 2) * CHUNK + (tile // 2) * 12 + part * SLAB + x


VMEM_LIMIT = 12 * 1024 * 1024


SPACE = {"vmem": pltpu.VMEM, "hbm": pltpu.HBM}


def kept_in(place, array):
    return pltpu.with_memory_space_constraint(array, SPACE[place]) if place in SPACE else array


class Fetched:
    def __init__(self, source, target, semaphore):
        self.target = target
        self.copy = pltpu.make_async_copy(source, target, semaphore)
        self.copy.start()
        self.pending = True

    def get(self):
        if self.pending:
            self.copy.wait()
            self.pending = False
        return self.target


class Ready:
    def __init__(self, ref):
        self.ref = ref

    def get(self):
        return self.ref


def call(kernel, out_shapes, scratch, args, interpret=False):
    places = [place for place, _ in args]
    arrays = [jnp.asarray(array) for _, array in args]
    specs = {
        "smem": pl.BlockSpec(memory_space=pltpu.SMEM),
        "vmem": pl.BlockSpec(memory_space=pltpu.VMEM),
        "hbm": pl.BlockSpec(memory_space=pltpu.HBM),
    }
    remote = [array for place, array in zip(places, arrays) if place == "hbm"]
    n_in, n_out = len(args), len(out_shapes)

    def entry(*refs):
        inputs, outputs = refs[:n_in], refs[n_in : n_in + n_out]
        rest = refs[n_in + n_out :]
        targets, semaphores, own_scratch = rest[: len(remote)], rest[len(remote)], rest[len(remote) + 1 :]
        handles, k = [], 0
        for place, ref in zip(places, inputs):
            if place == "hbm":
                handles.append(Fetched(ref, targets[k], semaphores.at[k]))
                k += 1
            else:
                handles.append(Ready(ref))
        for handle in handles:
            handle.get()
        kernel(*handles, *outputs, *own_scratch)

    return pl.pallas_call(
        entry,
        out_shape=out_shapes,
        in_specs=[specs[place] for place in places],
        out_specs=[specs["vmem"]] * n_out,
        scratch_shapes=[pltpu.VMEM(array.shape, array.dtype) for array in remote]
        + [pltpu.SemaphoreType.DMA((max(1, len(remote)),))]
        + scratch,
        interpret=interpret,
        compiler_params=pltpu.CompilerParams(vmem_limit_bytes=VMEM_LIMIT),
    )(*(kept_in(place, array) for place, array in zip(places, arrays)))


LOCAL = (("local", 0, 1),)
REMOTE = (("across", 1, 2), ("right", 0, 1), ("left", 0, 2))


def strided(part, x, s):
    return pl.ds(part * ROWS + x * 72 + s, 24, stride=3)


def density_kernel(tasks, members, where, hold, *refs):
    n = len(tasks)
    orbitals = refs[:members]
    z_table, y_table, out_ref, count_ref = refs[members:]
    kpair, _, _ = where()
    if hold:
        def step(i, carry):
            count_ref[0] = i
            return carry

        lax.fori_loop(0, jnp.where(kpair % 2 == 0, hold, 0), step, 0)
    lane = lane_index(24)
    lane16 = lane_index(16)
    for task, (kind, a, b) in enumerate(tasks):
        own_ref, far_ref = orbitals[a].get(), orbitals[b].get()
        for x in range(0, SLAB, 2):
            planes = []
            for v in (x, x + 1):
                tiles = ([], [])
                for s in range(3):
                    own_real, own_imag = own_ref[strided(0, v, s), :], own_ref[strided(1, v, s), :]
                    far_real, far_imag = far_ref[strided(0, v, s), :], far_ref[strided(1, v, s), :]
                    real = far_real * own_real + far_imag * own_imag
                    imag = far_real * own_imag - far_imag * own_real
                    if kind == "local":
                        packed = kpair % 2 == 1
                        real = jnp.where(packed, own_real * own_real + own_imag * own_imag, real)
                        imag = jnp.where(packed, far_real * far_real + far_imag * far_imag, imag)
                    tiles[0].append(real)
                    tiles[1].append(imag)
                parts = []
                for t0, t1, t2 in tiles:
                    rows = (
                        t0,
                        jnp.where(lane < 32, pltpu.roll(t0, 32, 1), pltpu.roll(t1, 32, 1)),
                        jnp.where(lane < 64, pltpu.roll(t1, 64, 1), pltpu.roll(t2, 64, 1)),
                        pltpu.roll(t2, 96, 1),
                    )
                    parts.append(jnp.concatenate(rows, axis=0))
                planes.append(jnp.concatenate(parts, axis=1))
            along_z = data_product(*split(jnp.concatenate(planes, axis=0)), z_table.get())
            columns = jnp.concatenate(
                [
                    jnp.concatenate(
                        [along_z[v * GRID : (v + 1) * GRID, c * LANES : (c + 1) * LANES] for c in range(2)], axis=0
                    )
                    for v in range(2)
                ],
                axis=1,
            )
            along_y = table_product(y_table.get()[...].reshape(4 * GRID, 2 * GRID), *split(columns))
            for v in range(2):
                for c in range(2):
                    bands = [
                        along_y[c * GRID + 16 * j : c * GRID + 16 * j + 16, v * LANES : (v + 1) * LANES]
                        for j in range(6)
                    ]
                    for tile in range(4):
                        band, start, _ = FILL[tile]
                        shift = (WIDTH[tile] - start) % LANES
                        value = jnp.where(lane16 < WIDTH[tile], bands[tile], pltpu.roll(bands[band], shift, 1))
                        row = task * 2 * CHUNK + chunk_row(tile, c, x + v)
                        out_ref[pl.ds(row, 16, stride=n * 2 * CHUNK), :] = value


def densities(tasks, orbitals, kept, early, hold=0, where=place, interpret=False):
    n = len(tasks)
    (out,) = call(
        lambda *refs: density_kernel(tasks, len(orbitals), where, hold, *refs),
        [kept((PENCILS * n * 2 * CHUNK, LANES), f32)],
        [pltpu.SMEM((1,), jnp.int32)],
        [*orbitals, (early, TABLES["forward_z"]), (early, TABLES["forward_y"])],
        interpret,
    )
    return out.reshape(PENCILS, n, 2, CHUNK, LANES)


def filter_kernel(groups, where, coords, *refs):
    chunks, (lanes, forward_table, inverse_table, out_ref) = refs[: len(groups)], refs[len(groups) :]
    coords_ref, lanes_ref = coords.get(), lanes.get()
    work = [(kind, chunks[g], i) for g, tasks in enumerate(groups) for i, (kind, _, _) in enumerate(tasks)]
    kpair, band, pencil = where()
    right, left = partners(kpair, band)
    points = {
        "local": (kpair, jnp.where(kpair % 2 == 1, kpair, kpair + 1)),
        "right": (kpair, right),
        "left": (kpair, left),
        "across": (right, left),
    }
    factor = (2.0 * math.pi / GRID) ** 2
    scale = -1.0 / (KPTS * NB) / GRID**3
    slot = lanes_ref[0:1, :]
    sign = (1 - 2 * (pencil % 2)).astype(f32)
    ky = sign * (8.0 * slot + (pencil // 2).astype(f32))
    ky = jnp.where(slot == jnp.where(pencil == 1, 0.0, -1.0), -48.0, ky)
    kz = lanes_ref[1:2, :]
    index = lax.broadcasted_iota(jnp.int32, (GRID, 2 * LANES), 0)
    kx = jnp.where(index < GRID // 2, index, index - GRID).astype(f32)
    for task, (kind, source, place) in enumerate(work):
        in_ref = source.get()
        here, there = points[kind]
        shift = [(coords_ref[here, a] - coords_ref[there, a]).astype(f32) * 0.25 for a in range(3)]
        plane = (ky + shift[1]) ** 2 + (kz + shift[2]) ** 2
        along_x = (kx + shift[0]) ** 2
        previous = None
        for h in range(2):
            rows = [
                in_ref[:, place, l, 8 * h : 8 * h + 16, :].reshape(256, LANES) for l in range(2)
            ]
            high, low = split(jnp.concatenate(rows, axis=1))
            forward_ref = forward_table.get()
            spectrum = table_product(forward_ref[h].reshape(4 * GRID, 256), high, low)
            squared = along_x + plane[:, h * 256 : (h + 1) * 256]
            coulomb = jnp.where(
                squared <= RADIUS * RADIUS, 4.0 * math.pi / (factor * squared + SCREENING), 0.0
            ) * scale
            spectrum = jnp.concatenate([spectrum[:GRID] * coulomb, spectrum[GRID:] * coulomb], axis=0)
            high, low = split(spectrum)
            inverse_ref = inverse_table.get()
            back = table_product(inverse_ref[h].reshape(512, 2 * GRID), high, low).reshape(PENCILS, 16, 2 * LANES)
            for l in range(2):
                part = back[:, :, l * LANES : (l + 1) * LANES]
                if h == 0:
                    out_ref[:, task, l, 0:8, :] = part[:, 0:8]
                else:
                    out_ref[:, task, l, 16:24, :] = part[:, 8:16]
                    out_ref[:, task, l, 8:16, :] = part[:, 0:8] + previous[:, 8:16, l * LANES : (l + 1) * LANES]
            previous = back


def filtered(groups, coords, chunks, where=place, interpret=False):
    n = sum(len(tasks) for tasks in groups)
    (out,) = call(
        lambda *refs: filter_kernel(groups, where, *refs),
        [jax.ShapeDtypeStruct((PENCILS, n, 2, CHUNK, LANES), f32)],
        [],
        [
            ("smem", coords),
            *chunks,
            ("vmem", TABLES["lanes"]),
            ("vmem", TABLES["forward_x"]),
            ("vmem", TABLES["inverse_x"]),
        ],
        interpret,
    )
    return out


def potential_kernel(tasks, first, n, members, bases, where, chunks, *refs):
    in_ref = chunks.get()
    orbitals, refs = refs[:members], refs[members:]
    y_table, z_table, refs = refs[0], refs[1], refs[2:]
    started, sum_refs = refs[:bases], refs[bases:]
    earlier = dict(enumerate(started))
    kpair, _, _ = where()
    lane = lane_index(24)
    lane16 = lane_index(16)
    for task, (kind, a, b) in enumerate(tasks, first):
        for x in range(0, SLAB, 2):
            pair = []
            for v in (x, x + 1):
                parts = []
                for c in range(2):
                    tiles = [
                        in_ref[pl.ds(task * 2 * CHUNK + chunk_row(t, c, v), 16, stride=n * 2 * CHUNK), :]
                        for t in range(4)
                    ]
                    bands = [jnp.where(lane16 < WIDTH[t], tiles[t], 0.0) for t in range(4)]
                    for (ta, tb) in ((3, 0), (1, 2)):
                        _, sa, ca = FILL[ta]
                        _, sb, cb = FILL[tb]
                        head = pltpu.roll(tiles[ta], (sa - WIDTH[ta]) % LANES, 1)
                        tail = pltpu.roll(tiles[tb], (sb - WIDTH[tb]) % LANES, 1)
                        bands.append(jnp.where(lane16 < ca, head, jnp.where(lane16 < ca + cb, tail, 0.0)))
                    parts += bands
                pair.append(jnp.concatenate(parts, axis=0))
            columns = jnp.concatenate(pair, axis=1)
            along_y = table_product(y_table.get()[...].reshape(4 * GRID, 2 * GRID), *split(columns))
            planes = jnp.concatenate(
                [
                    jnp.concatenate(
                        [along_y[c * GRID : (c + 1) * GRID, v * LANES : (v + 1) * LANES] for c in range(2)], axis=1
                    )
                    for v in range(2)
                ],
                axis=0,
            )
            along_z = data_product(*split(planes), z_table.get())
            own_ref, far_ref = orbitals[a].get(), orbitals[b].get()
            for v in range(2):
                tiles = []
                for c in range(2):
                    v0, v1, v2, v3 = (
                        along_z[v * GRID + 24 * j : v * GRID + 24 * j + 24, c * LANES : (c + 1) * LANES]
                        for j in range(4)
                    )
                    v1, v2, v3 = pltpu.roll(v1, 96, 1), pltpu.roll(v2, 64, 1), pltpu.roll(v3, 32, 1)
                    tiles.append(
                        (jnp.where(lane < 96, v0, v1), jnp.where(lane < 64, v1, v2), jnp.where(lane < 32, v2, v3))
                    )
                for s in range(3):
                    at_real, at_imag = strided(0, x + v, s), strided(1, x + v, s)
                    own_real, own_imag = own_ref[at_real, :], own_ref[at_imag, :]
                    far_real, far_imag = far_ref[at_real, :], far_ref[at_imag, :]
                    pot_real, pot_imag = tiles[0][s], tiles[1][s]
                    here_real = far_real * pot_real - far_imag * pot_imag
                    here_imag = far_real * pot_imag + far_imag * pot_real
                    there_real = own_real * pot_real + own_imag * pot_imag
                    there_imag = own_imag * pot_real - own_real * pot_imag
                    if kind == "local":
                        packed = kpair % 2 == 1
                        here_real = jnp.where(packed, own_real * pot_real, here_real)
                        here_imag = jnp.where(packed, own_imag * pot_real, here_imag)
                        there_real = jnp.where(packed, far_real * pot_imag, there_real)
                        there_imag = jnp.where(packed, far_imag * pot_imag, there_imag)
                    for member, real, imag in ((a, here_real, here_imag), (b, there_real, there_imag)):
                        if member in earlier:
                            base_ref = earlier[member].get()
                            real = real + base_ref[at_real, :]
                            imag = imag + base_ref[at_imag, :]
                        sum_refs[member][at_real, :] = real
                        sum_refs[member][at_imag, :] = imag
        for member in (a, b):
            earlier[member] = Ready(sum_refs[member])


def potentials(tasks, first, chunks, orbitals, kept, early, bases=(), where=place, interpret=False):
    n = chunks.shape[1]
    return call(
        lambda *refs: potential_kernel(tasks, first, n, len(orbitals), len(bases), where, *refs),
        kept,
        [],
        [
            ("vmem", chunks.reshape(PENCILS * n * 2 * CHUNK, LANES)),
            *orbitals,
            (early, TABLES["inverse_y"]),
            (early, TABLES["inverse_z"]),
            *bases,
        ],
        interpret,
    )


def line(chip, core):
    chip %= 4
    return (chip // 2) * 4 + core * 2 + chip % 2


TURN = (1, 0, 0, 0)


def route(kind):
    pairs = []
    for chip in range(4):
        for core in range(2):
            if kind == "local":
                source = line(chip, 1 - core)
            elif kind == "right":
                source = line(chip + 1, core ^ TURN[chip])
            else:
                source = line(chip - 1, core ^ (1 - TURN[chip - 1]))
            pairs.append((source, line(chip, core)))
    return pairs


def fetch(kind, block):
    return lax.ppermute(block, ("kpair", "band"), route(kind))


def give_back(kind, block):
    return lax.ppermute(block, ("kpair", "band"), [(b, a) for a, b in route(kind)])


def transpose(chunks):
    return lax.all_to_all(chunks, "pencil", 0, 0, tiled=True)


DENSE = (2 * ROWS, LANES)
HOLD = 1100


def body(orbitals, kcoords):
    own = orbitals.reshape(DENSE)
    right, left, other = fetch("right", own), fetch("left", own), fetch("local", own)
    near = [("hbm", own), ("vmem", other)]
    far = [("vmem", own), ("vmem", right), ("vmem", left)]
    chunks_near = densities(LOCAL, near, pltpu.HBM, "hbm", HOLD)
    sent_near = transpose(chunks_near)
    chunks_far = densities(REMOTE, far, jax.ShapeDtypeStruct, "vmem")
    sent_far = transpose(chunks_far)
    spectrum = filtered((REMOTE, LOCAL), kcoords, [("vmem", sent_far), ("vmem", sent_near)])
    back = transpose(spectrum)
    kept = [jax.ShapeDtypeStruct(DENSE, f32)] * 3
    far_sum, for_right, for_left = potentials(REMOTE, 0, back, far, kept, "vmem")
    from_right = give_back("right", for_right)
    from_left = give_back("left", for_left)
    kept = [jax.ShapeDtypeStruct(DENSE, f32)] * 2
    own_sum, for_other = potentials(LOCAL, len(REMOTE), back, near, kept, "hbm", [("vmem", far_sum)])
    from_other = give_back("local", for_other)
    out = own_sum + from_other + (from_right + from_left)
    return out.reshape(2, 1, 1, SLAB, GRID * GRID)


def solution(mesh):
    in_specs = (P(None, "kpair", "band", "pencil", None), P())
    out_specs = P(None, "kpair", "band", "pencil", None)
    return jax.shard_map(body, mesh=mesh, in_specs=in_specs, out_specs=out_specs, check_vma=False)
```

```python
import math

import jax
import jax.numpy as jnp
import numpy as np
from jax import lax
from jax.experimental import pallas as pl
from jax.experimental.pallas import tpu as pltpu
from jax.sharding import PartitionSpec as P

GRID = 96
NB = 2
KPTS = 4
SCREENING = 0.5
RADIUS = GRID // 2 - 1
PENCILS = 16
SLAB = GRID // PENCILS
LANES = 128
ROWS = SLAB * GRID * GRID // LANES
CHUNK = 24

f32 = jnp.float32
bf16 = jnp.bfloat16

KZ = np.array([0] + [s * i for i in range(1, 48) for s in (1, -1)])
KY = np.array([[(8 * j + d // 2) * (1 - 2 * (d % 2)) for d in range(16)] for j in range(6)])
KY[0, 1] = -48
WIDTH = [
    2 * min(RADIUS, int(0.75 + math.sqrt(RADIUS**2 - max(0.0, 8 * j - 0.75) ** 2))) + 1
    for j in range(6)
]
SPLIT4 = LANES - WIDTH[3]
SPLIT5 = LANES - WIDTH[1]
FILL = {
    3: (4, 0, SPLIT4),
    0: (4, SPLIT4, WIDTH[4] - SPLIT4),
    1: (5, 0, SPLIT5),
    2: (5, SPLIT5, WIDTH[5] - SPLIT5),
}
for tile, (band, first, count) in FILL.items():
    assert WIDTH[tile] + count <= LANES


def split(values):
    high = jnp.asarray(values, f32).astype(bf16)
    low = (jnp.asarray(values, f32) - high.astype(f32)).astype(bf16)
    return high, low


def halves(table):
    table = np.asarray(table, np.float32)
    high = table.astype(bf16)
    low = (table - high.astype(np.float32)).astype(bf16)
    return np.stack([high, low])


def angles(rows, cols):
    product = np.outer(rows, cols) % GRID
    angle = product * (2.0 * math.pi / GRID)
    return np.cos(angle), np.sin(angle)


def build_tables():
    cosine, sine = angles(np.arange(GRID), KZ)
    forward_z = np.zeros((2, LANES, 2, LANES))
    inverse_z = np.zeros((2, LANES, 2, LANES))
    n = len(KZ)
    forward_z[0, :GRID, 0, :n] = cosine
    forward_z[1, :GRID, 0, :n] = sine
    forward_z[0, :GRID, 1, :n] = -sine
    forward_z[1, :GRID, 1, :n] = cosine
    inverse_z[0, :n, 0, :GRID] = cosine.T
    inverse_z[1, :n, 0, :GRID] = -sine.T
    inverse_z[0, :n, 1, :GRID] = sine.T
    inverse_z[1, :n, 1, :GRID] = cosine.T
    order_y = np.array([4 * g + j for j in range(4) for g in range(24)])
    cosine, sine = angles(KY.reshape(-1), order_y)
    forward_y = np.block([[cosine, sine], [-sine, cosine]])
    inverse_y = np.block([[cosine.T, -sine.T], [sine.T, cosine.T]])
    freq = np.where(np.arange(GRID) < GRID // 2, np.arange(GRID), np.arange(GRID) - GRID)
    cosine, sine = angles(freq, np.arange(GRID))
    full_f = np.block([[cosine, sine], [-sine, cosine]])
    full_i = np.block([[cosine.T, -sine.T], [sine.T, cosine.T]])
    forward_x = np.zeros((2, 2 * GRID, PENCILS, 16))
    inverse_x = np.zeros((2, PENCILS, 16, 2 * GRID))
    for h in range(2):
        for s in range(PENCILS):
            for c in range(2):
                rows = slice(4 * h + c * SLAB, 4 * h + (c + 1) * SLAB)
                xs = slice(c * GRID + s * SLAB, c * GRID + (s + 1) * SLAB)
                forward_x[h, :, s, rows] = full_f[:, xs]
                inverse_x[h, s, rows, :] = full_i[xs, :]
    lanes = np.zeros((8, 4 * LANES), np.float32)
    lanes[1] = 1000.0
    for tile in range(4):
        base = tile * LANES
        lanes[0, base : base + WIDTH[tile]] = tile
        lanes[1, base : base + WIDTH[tile]] = KZ[: WIDTH[tile]]
        band, first, count = FILL[tile]
        base += WIDTH[tile]
        lanes[0, base : base + count] = band
        lanes[1, base : base + count] = KZ[first : first + count]
    return dict(
        forward_z=halves(forward_z.reshape(2 * LANES, 2 * LANES)),
        inverse_z=halves(inverse_z.reshape(2 * LANES, 2 * LANES)),
        forward_y=halves(forward_y),
        inverse_y=halves(inverse_y),
        forward_x=halves(forward_x.reshape(2, 2 * GRID, 256)).swapaxes(0, 1),
        inverse_x=halves(inverse_x.reshape(2, 256, 2 * GRID)).swapaxes(0, 1),
        lanes=lanes,
    )


TABLES = build_tables()


def place():
    kpair = lax.axis_index("kpair")
    band = lax.axis_index("band")
    pencil = lax.axis_index("pencil")
    return kpair, band, pencil


def partners(kpair, band):
    core = kpair % 2
    chip = (kpair // 2) * 2 + band
    right_core = jnp.where(chip == 0, 1 - core, core)
    left_core = jnp.where(chip == 1, core, 1 - core)
    right = ((chip + 1) % 4 // 2) * 2 + right_core
    left = ((chip + 3) % 4 // 2) * 2 + left_core
    return right, left


def data_product(left_high, left_low, table_ref):
    rows = left_high.shape[0]
    dot = lambda a, b: jnp.dot(a, b, preferred_element_type=f32)
    both = dot(jnp.concatenate([left_high, left_low], axis=0), table_ref[0])
    return both[:rows] + (both[rows:] + dot(left_high, table_ref[1]))


def table_product(table, right_high, right_low):
    rows = table.shape[0] // 2
    dot = lambda a, b: jnp.dot(a, b, preferred_element_type=f32)
    both = dot(table, right_high)
    return both[:rows] + (both[rows:] + dot(table[:rows], right_low))


def lane_index(rows):
    return lax.broadcasted_iota(jnp.int32, (rows, LANES), 1)


def chunk_row(tile, part, x):
    return (tile % 2) * CHUNK + (tile // 2) * 12 + part * SLAB + x


VMEM_LIMIT = 12 * 1024 * 1024


SPACE = {"vmem": pltpu.VMEM, "hbm": pltpu.HBM}


def kept_in(place, array):
    return pltpu.with_memory_space_constraint(array, SPACE[place]) if place in SPACE else array


class Fetched:
    def __init__(self, source, target, semaphore):
        self.target = target
        self.copy = pltpu.make_async_copy(source, target, semaphore)
        self.copy.start()
        self.pending = True

    def get(self):
        if self.pending:
            self.copy.wait()
            self.pending = False
        return self.target


class Ready:
    def __init__(self, ref):
        self.ref = ref

    def get(self):
        return self.ref


def call(kernel, out_shapes, scratch, args, interpret=False):
    places = [place for place, _ in args]
    arrays = [jnp.asarray(array) for _, array in args]
    specs = {
        "smem": pl.BlockSpec(memory_space=pltpu.SMEM),
        "vmem": pl.BlockSpec(memory_space=pltpu.VMEM),
        "hbm": pl.BlockSpec(memory_space=pltpu.HBM),
    }
    remote = [array for place, array in zip(places, arrays) if place == "hbm"]
    n_in, n_out = len(args), len(out_shapes)

    def entry(*refs):
        inputs, outputs = refs[:n_in], refs[n_in : n_in + n_out]
        rest = refs[n_in + n_out :]
        targets, semaphores, own_scratch = rest[: len(remote)], rest[len(remote)], rest[len(remote) + 1 :]
        handles, k = [], 0
        for place, ref in zip(places, inputs):
            if place == "hbm":
                handles.append(Fetched(ref, targets[k], semaphores.at[k]))
                k += 1
            else:
                handles.append(Ready(ref))
        for handle in handles:
            handle.get()
        kernel(*handles, *outputs, *own_scratch)

    return pl.pallas_call(
        entry,
        out_shape=out_shapes,
        in_specs=[specs[place] for place in places],
        out_specs=[specs["vmem"]] * n_out,
        scratch_shapes=[pltpu.VMEM(array.shape, array.dtype) for array in remote]
        + [pltpu.SemaphoreType.DMA((max(1, len(remote)),))]
        + scratch,
        interpret=interpret,
        compiler_params=pltpu.CompilerParams(vmem_limit_bytes=VMEM_LIMIT),
    )(*(kept_in(place, array) for place, array in zip(places, arrays)))


LOCAL = (("local", 0, 1),)
REMOTE = (("across", 1, 2), ("right", 0, 1), ("left", 0, 2))


def in_stages(work, first, second, depth):
    waiting = []
    for item in work:
        waiting.append((*item, first(*item)))
        if len(waiting) > depth:
            second(*waiting.pop(0))
    for item in waiting:
        second(*item)


def strided(part, x, s):
    return pl.ds(part * ROWS + x * 72 + s, 24, stride=3)


def density_kernel(tasks, members, where, hold, *refs):
    n = len(tasks)
    orbitals = refs[:members]
    z_table, y_table, out_ref, count_ref = refs[members:]
    kpair, _, _ = where()
    if hold:
        def step(i, carry):
            count_ref[0] = i
            return carry

        lax.fori_loop(0, jnp.where(kpair % 2 == 0, hold, 0), step, 0)
    lane = lane_index(24)
    lane16 = lane_index(16)

    def transform_z(task, x):
            kind, a, b = tasks[task]
            own_ref, far_ref = orbitals[a].get(), orbitals[b].get()
            planes = []
            for v in (x, x + 1):
                tiles = ([], [])
                for s in range(3):
                    own_real, own_imag = own_ref[strided(0, v, s), :], own_ref[strided(1, v, s), :]
                    far_real, far_imag = far_ref[strided(0, v, s), :], far_ref[strided(1, v, s), :]
                    real = far_real * own_real + far_imag * own_imag
                    imag = far_real * own_imag - far_imag * own_real
                    if kind == "local":
                        packed = kpair % 2 == 1
                        real = jnp.where(packed, own_real * own_real + own_imag * own_imag, real)
                        imag = jnp.where(packed, far_real * far_real + far_imag * far_imag, imag)
                    tiles[0].append(real)
                    tiles[1].append(imag)
                parts = []
                for t0, t1, t2 in tiles:
                    rows = (
                        t0,
                        jnp.where(lane < 32, pltpu.roll(t0, 32, 1), pltpu.roll(t1, 32, 1)),
                        jnp.where(lane < 64, pltpu.roll(t1, 64, 1), pltpu.roll(t2, 64, 1)),
                        pltpu.roll(t2, 96, 1),
                    )
                    parts.append(jnp.concatenate(rows, axis=0))
                planes.append(jnp.concatenate(parts, axis=1))
            along_z = data_product(*split(jnp.concatenate(planes, axis=0)), z_table.get())
            return along_z

    def transform_y(task, x, along_z):
            columns = jnp.concatenate(
                [
                    jnp.concatenate(
                        [along_z[v * GRID : (v + 1) * GRID, c * LANES : (c + 1) * LANES] for c in range(2)], axis=0
                    )
                    for v in range(2)
                ],
                axis=1,
            )
            along_y = table_product(y_table.get()[...].reshape(4 * GRID, 2 * GRID), *split(columns))
            for v in range(2):
                for c in range(2):
                    bands = [
                        along_y[c * GRID + 16 * j : c * GRID + 16 * j + 16, v * LANES : (v + 1) * LANES]
                        for j in range(6)
                    ]
                    for tile in range(4):
                        band, start, _ = FILL[tile]
                        shift = (WIDTH[tile] - start) % LANES
                        value = jnp.where(lane16 < WIDTH[tile], bands[tile], pltpu.roll(bands[band], shift, 1))
                        row = task * 2 * CHUNK + chunk_row(tile, c, x + v)
                        out_ref[pl.ds(row, 16, stride=n * 2 * CHUNK), :] = value

    in_stages([(task, x) for task in range(n) for x in range(0, SLAB, 2)], transform_z, transform_y, 2)


def densities(tasks, orbitals, kept, early, hold=0, where=place, interpret=False):
    n = len(tasks)
    (out,) = call(
        lambda *refs: density_kernel(tasks, len(orbitals), where, hold, *refs),
        [kept((PENCILS * n * 2 * CHUNK, LANES), f32)],
        [pltpu.SMEM((1,), jnp.int32)],
        [*orbitals, (early, TABLES["forward_z"]), (early, TABLES["forward_y"])],
        interpret,
    )
    return out.reshape(PENCILS, n, 2, CHUNK, LANES)


def filter_kernel(groups, where, coords, *refs):
    chunks, (lanes, forward_table, inverse_table, out_ref) = refs[: len(groups)], refs[len(groups) :]
    coords_ref, lanes_ref = coords.get(), lanes.get()
    work = [(kind, chunks[g], i) for g, tasks in enumerate(groups) for i, (kind, _, _) in enumerate(tasks)]
    kpair, band, pencil = where()
    right, left = partners(kpair, band)
    points = {
        "local": (kpair, jnp.where(kpair % 2 == 1, kpair, kpair + 1)),
        "right": (kpair, right),
        "left": (kpair, left),
        "across": (right, left),
    }
    factor = (2.0 * math.pi / GRID) ** 2
    scale = -1.0 / (KPTS * NB) / GRID**3
    slot = lanes_ref[0:1, :]
    sign = (1 - 2 * (pencil % 2)).astype(f32)
    ky = sign * (8.0 * slot + (pencil // 2).astype(f32))
    ky = jnp.where(slot == jnp.where(pencil == 1, 0.0, -1.0), -48.0, ky)
    kz = lanes_ref[1:2, :]
    index = lax.broadcasted_iota(jnp.int32, (GRID, 2 * LANES), 0)
    kx = jnp.where(index < GRID // 2, index, index - GRID).astype(f32)

    def forward(task):
        _, source, place = work[task]
        in_ref = source.get()
        spectra = []
        for h in range(2):
            rows = [in_ref[:, place, l, 8 * h : 8 * h + 16, :].reshape(256, LANES) for l in range(2)]
            high, low = split(jnp.concatenate(rows, axis=1))
            spectra.append(table_product(forward_table.get()[h].reshape(4 * GRID, 256), high, low))
        return spectra

    def inverse(task, spectra):
        kind, _, _ = work[task]
        here, there = points[kind]
        shift = [(coords_ref[here, a] - coords_ref[there, a]).astype(f32) * 0.25 for a in range(3)]
        plane = (ky + shift[1]) ** 2 + (kz + shift[2]) ** 2
        along_x = (kx + shift[0]) ** 2
        backs = []
        for h in range(2):
            squared = along_x + plane[:, h * 256 : (h + 1) * 256]
            coulomb = jnp.where(
                squared <= RADIUS * RADIUS, 4.0 * math.pi / (factor * squared + SCREENING), 0.0
            ) * scale
            spectrum = jnp.concatenate([spectra[h][:GRID] * coulomb, spectra[h][GRID:] * coulomb], axis=0)
            back = table_product(inverse_table.get()[h].reshape(512, 2 * GRID), *split(spectrum))
            backs.append(back.reshape(PENCILS, 16, 2 * LANES))
        for l in range(2):
            low, high = (back[:, :, l * LANES : (l + 1) * LANES] for back in backs)
            out_ref[:, task, l, 0:8, :] = low[:, 0:8]
            out_ref[:, task, l, 8:16, :] = low[:, 8:16] + high[:, 0:8]
            out_ref[:, task, l, 16:24, :] = high[:, 8:16]

    in_stages([(task,) for task in range(len(work))], forward, inverse, 1)


def filtered(groups, coords, chunks, where=place, interpret=False):
    n = sum(len(tasks) for tasks in groups)
    (out,) = call(
        lambda *refs: filter_kernel(groups, where, *refs),
        [jax.ShapeDtypeStruct((PENCILS, n, 2, CHUNK, LANES), f32)],
        [],
        [
            ("smem", coords),
            *chunks,
            ("vmem", TABLES["lanes"]),
            ("vmem", TABLES["forward_x"]),
            ("vmem", TABLES["inverse_x"]),
        ],
        interpret,
    )
    return out


def potential_kernel(tasks, first, n, members, bases, where, chunks, *refs):
    in_ref = chunks.get()
    orbitals, refs = refs[:members], refs[members:]
    y_table, z_table, refs = refs[0], refs[1], refs[2:]
    started, sum_refs = refs[:bases], refs[bases:]
    kpair, _, _ = where()
    lane = lane_index(24)
    lane16 = lane_index(16)

    def base_of(task, member):
        if any(member in tasks[t][1:] for t in range(task - first)):
            return Ready(sum_refs[member])
        return started[member] if member < bases else None

    def transform_y(task, x):
            pair = []
            for v in (x, x + 1):
                parts = []
                for c in range(2):
                    tiles = [
                        in_ref[pl.ds(task * 2 * CHUNK + chunk_row(t, c, v), 16, stride=n * 2 * CHUNK), :]
                        for t in range(4)
                    ]
                    bands = [jnp.where(lane16 < WIDTH[t], tiles[t], 0.0) for t in range(4)]
                    for (ta, tb) in ((3, 0), (1, 2)):
                        _, sa, ca = FILL[ta]
                        _, sb, cb = FILL[tb]
                        head = pltpu.roll(tiles[ta], (sa - WIDTH[ta]) % LANES, 1)
                        tail = pltpu.roll(tiles[tb], (sb - WIDTH[tb]) % LANES, 1)
                        bands.append(jnp.where(lane16 < ca, head, jnp.where(lane16 < ca + cb, tail, 0.0)))
                    parts += bands
                pair.append(jnp.concatenate(parts, axis=0))
            columns = jnp.concatenate(pair, axis=1)
            along_y = table_product(y_table.get()[...].reshape(4 * GRID, 2 * GRID), *split(columns))
            planes = jnp.concatenate(
                [
                    jnp.concatenate(
                        [along_y[c * GRID : (c + 1) * GRID, v * LANES : (v + 1) * LANES] for c in range(2)], axis=1
                    )
                    for v in range(2)
                ],
                axis=0,
            )
            return planes

    def transform_z(task, x, planes):
            kind, a, b = tasks[task - first]
            along_z = data_product(*split(planes), z_table.get())
            own_ref, far_ref = orbitals[a].get(), orbitals[b].get()
            for v in range(2):
                tiles = []
                for c in range(2):
                    v0, v1, v2, v3 = (
                        along_z[v * GRID + 24 * j : v * GRID + 24 * j + 24, c * LANES : (c + 1) * LANES]
                        for j in range(4)
                    )
                    v1, v2, v3 = pltpu.roll(v1, 96, 1), pltpu.roll(v2, 64, 1), pltpu.roll(v3, 32, 1)
                    tiles.append(
                        (jnp.where(lane < 96, v0, v1), jnp.where(lane < 64, v1, v2), jnp.where(lane < 32, v2, v3))
                    )
                for s in range(3):
                    at_real, at_imag = strided(0, x + v, s), strided(1, x + v, s)
                    own_real, own_imag = own_ref[at_real, :], own_ref[at_imag, :]
                    far_real, far_imag = far_ref[at_real, :], far_ref[at_imag, :]
                    pot_real, pot_imag = tiles[0][s], tiles[1][s]
                    here_real = far_real * pot_real - far_imag * pot_imag
                    here_imag = far_real * pot_imag + far_imag * pot_real
                    there_real = own_real * pot_real + own_imag * pot_imag
                    there_imag = own_imag * pot_real - own_real * pot_imag
                    if kind == "local":
                        packed = kpair % 2 == 1
                        here_real = jnp.where(packed, own_real * pot_real, here_real)
                        here_imag = jnp.where(packed, own_imag * pot_real, here_imag)
                        there_real = jnp.where(packed, far_real * pot_imag, there_real)
                        there_imag = jnp.where(packed, far_imag * pot_imag, there_imag)
                    for member, real, imag in ((a, here_real, here_imag), (b, there_real, there_imag)):
                        base = base_of(task, member)
                        if base is not None:
                            base_ref = base.get()
                            real = real + base_ref[at_real, :]
                            imag = imag + base_ref[at_imag, :]
                        sum_refs[member][at_real, :] = real
                        sum_refs[member][at_imag, :] = imag

    work = [(task, x) for task in range(first, first + len(tasks)) for x in range(0, SLAB, 2)]
    in_stages(work, transform_y, transform_z, 2)


def potentials(tasks, first, chunks, orbitals, kept, early, bases=(), where=place, interpret=False):
    n = chunks.shape[1]
    return call(
        lambda *refs: potential_kernel(tasks, first, n, len(orbitals), len(bases), where, *refs),
        kept,
        [],
        [
            ("vmem", chunks.reshape(PENCILS * n * 2 * CHUNK, LANES)),
            *orbitals,
            (early, TABLES["inverse_y"]),
            (early, TABLES["inverse_z"]),
            *bases,
        ],
        interpret,
    )


def line(chip, core):
    chip %= 4
    return (chip // 2) * 4 + core * 2 + chip % 2


TURN = (1, 0, 0, 0)


def route(kind):
    pairs = []
    for chip in range(4):
        for core in range(2):
            if kind == "local":
                source = line(chip, 1 - core)
            elif kind == "right":
                source = line(chip + 1, core ^ TURN[chip])
            else:
                source = line(chip - 1, core ^ (1 - TURN[chip - 1]))
            pairs.append((source, line(chip, core)))
    return pairs


def fetch(kind, block):
    return lax.ppermute(block, ("kpair", "band"), route(kind))


def give_back(kind, block):
    return lax.ppermute(block, ("kpair", "band"), [(b, a) for a, b in route(kind)])


def transpose(chunks):
    return lax.all_to_all(chunks, "pencil", 0, 0, tiled=True)


DENSE = (2 * ROWS, LANES)
HOLD = 1100


def body(orbitals, kcoords):
    own = orbitals.reshape(DENSE)
    right, left, other = fetch("right", own), fetch("left", own), fetch("local", own)
    near = [("hbm", own), ("vmem", other)]
    far = [("vmem", own), ("vmem", right), ("vmem", left)]
    chunks_near = densities(LOCAL, near, pltpu.HBM, "hbm", HOLD)
    sent_near = transpose(chunks_near)
    chunks_far = densities(REMOTE, far, jax.ShapeDtypeStruct, "vmem")
    sent_far = transpose(chunks_far)
    spectrum = filtered((REMOTE, LOCAL), kcoords, [("vmem", sent_far), ("vmem", sent_near)])
    back = transpose(spectrum)
    kept = [jax.ShapeDtypeStruct(DENSE, f32)] * 3
    far_sum, for_right, for_left = potentials(REMOTE, 0, back, far, kept, "vmem")
    from_right = give_back("right", for_right)
    from_left = give_back("left", for_left)
    kept = [jax.ShapeDtypeStruct(DENSE, f32)] * 2
    own_sum, for_other = potentials(
        LOCAL, len(REMOTE), back, [("hbm", own), ("hbm", other)], kept, "hbm", [("vmem", far_sum)]
    )
    from_other = give_back("local", for_other)
    out = own_sum + from_other + (from_right + from_left)
    return out.reshape(2, 1, 1, SLAB, GRID * GRID)


def solution(mesh):
    in_specs = (P(None, "kpair", "band", "pencil", None), P())
    out_specs = P(None, "kpair", "band", "pencil", None)
    return jax.shard_map(body, mesh=mesh, in_specs=in_specs, out_specs=out_specs, check_vma=False)
```
